32 devices in a mesh: dp: 2 (over x), seq: 16 (over z, y, core).
Axes of the slice: x: 2, y: 2, z: 4, core: 2. Of those that a mesh axis runs over, the one named last changes fastest.
Arguments:
- query: bfloat16 [2048, 3072], P('seq', 'dp'), may hold values from -300 to 300
- key: bfloat16 [2048, 3072], P('seq', 'dp'), may hold values from -10 to 10
- value: bfloat16 [2048, 3072], P('seq', 'dp'), may hold values from -6 to 6
- d_query: bfloat16 [2048, 3072], P('seq', 'dp'), may hold values from -6 to 6
- d_key: bfloat16 [2048, 3072], P('seq', 'dp'), may hold values from -6 to 6
- d_value: bfloat16 [2048, 3072], P('seq', 'dp'), may hold values from -6 to 6
- residual: bfloat16 [2048, 3072], P('seq', 'dp'), may hold values from -6 to 6
- d_residual: bfloat16 [2048, 3072], P('seq', 'dp'), may hold values from -6 to 6
- w_in: bfloat16 [3072, 7168], P('seq', 'dp'), may hold values from -0.109375 to 0.109375
- w_out: bfloat16 [7168, 3072], P(('dp', 'seq')), may hold values from -0.125 to 0.125
Outputs:
- block_out: bfloat16 [2048, 3072], P('seq', 'dp')
- d_block_out: bfloat16 [2048, 3072], P('seq', 'dp')
The draws below stay inside these ranges and needn't reach their ends.
All inputs are finite; a program needn't handle non-finite values.
Results may differ from the reference program's by a relative error of at most 0.025.
Values may be sent and summed in bfloat16 or wider, within the bound.
A program may use at most 192 MiB of HBM per device.

```python
import jax
import jax.numpy as jnp
from jax import lax

HEAD_DIM = 128
HEADS = 24
D = 3072
FF = 7168
LENGTH = 2048


def joint_draw(base_key):
    folded = jax.random.fold_in(base_key, 11)
    key_a, key_b = jax.random.split(folded, 2)
    keys_arr = jnp.clip(jax.random.normal(key_a, (LENGTH, D), jnp.float32), -5.0, 5.0)
    queries = jnp.clip(jax.random.normal(key_b, (LENGTH, D), jnp.float32), -5.0, 5.0)
    return (queries, keys_arr)


def draw_query(base_key, part):
    return joint_draw(base_key)[0].astype(jnp.bfloat16)


def draw_key(base_key, part):
    return joint_draw(base_key)[1].astype(jnp.bfloat16)


def raised(values, key, source, target, parts, factor):
    owner, partner = [(jnp.arange(values.shape[position]) // (values.shape[position] // parts)).reshape([-1 if axis == position else 1 for axis in range(values.ndim)]) for position in (source, target)]
    chosen = jax.random.permutation(key, parts)[partner]
    strong = (owner == chosen) | (owner == (partner + parts // 2) % parts)
    return jnp.where(strong, factor * values, values)


def shard_levels(rng, shape, cuts, low, top_value):
    loudness = 1.0
    for position, blocks in cuts:
        draws = jax.random.uniform(jax.random.fold_in(jax.random.fold_in(rng, 6), position), (blocks,), jnp.float32, low / len(cuts), top_value / len(cuts))
        loudness = loudness * jnp.repeat(jnp.exp(draws), shape[position] // blocks).reshape((-1,) + (1,) * (len(shape) - 1 - position))
    return loudness


def scatter_about(rng, shape, deviation, bound, pieces=(), dtype=jnp.bfloat16):
    entries = deviation * jax.random.normal(rng, shape, jnp.float32)
    if pieces:
        entries = entries * shard_levels(rng, shape, pieces, -0.22, 0.18)
    return jnp.clip(entries, -bound, bound).astype(dtype)


def heavy_noise(rng, extent, spread, bound, pieces, heavy, held_as=jnp.bfloat16):
    result = spread * jax.random.normal(rng, extent, jnp.float32)
    if pieces:
        result = result * shard_levels(rng, extent, pieces, -0.22, 0.18)
    return jnp.clip(raised(result, jax.random.fold_in(rng, 3), *heavy), -bound, bound).astype(held_as)


def setup_inputs(seed: int = 0) -> dict:
    keys = jax.random.split(jax.random.key(seed), 11)
    query = draw_query(jax.random.fold_in(keys[10], 71), 0)
    key = draw_key(jax.random.fold_in(keys[10], 71), 0)
    value = scatter_about(keys[2], (LENGTH, D), 1.0, 6.0, ((0, 16), (1, 2)))
    d_query = scatter_about(keys[3], (LENGTH, D), 1.0, 6.0, ((0, 16), (1, 2)))
    d_key = scatter_about(keys[4], (LENGTH, D), 1.0, 6.0, ((0, 16), (1, 2)))
    d_value = scatter_about(keys[5], (LENGTH, D), 1.0, 6.0, ((0, 16), (1, 2)))
    residual = scatter_about(keys[6], (LENGTH, D), 1.0, 6.0, ((0, 16), (1, 2)))
    d_residual = scatter_about(keys[7], (LENGTH, D), 1.0, 6.0, ((0, 16), (1, 2)))
    w_in = scatter_about(keys[8], (D, FF), D ** -0.5, 0.109375, ((0, 16), (1, 2)))
    w_out = heavy_noise(keys[9], (FF, D), FF ** -0.5, 0.125, ((0, 32),), (0, 1, 32, 2.75))
    return dict(query=query, key=key, value=value, d_query=d_query, d_key=d_key, d_value=d_value, residual=residual, d_residual=d_residual, w_in=w_in, w_out=w_out)


gelu_coeff = 0.7978845608
cubic_coeff = 0.044715

def gelu_pair(pre_act, d_pre_act):
    inner_arg = gelu_coeff * (pre_act + cubic_coeff * pre_act * pre_act * pre_act)
    hyper = jnp.tanh(inner_arg)
    gelu_value = 0.5 * pre_act * (1.0 + hyper)
    gelu_slope = 0.5 * (1.0 + hyper) + 0.5 * pre_act * (1.0 - hyper * hyper) * gelu_coeff * (1.0 + 3.0 * cubic_coeff * pre_act * pre_act)
    return (gelu_value, gelu_slope * d_pre_act)

def head_attend(operands):
    query_head, key_head, value_head, dquery_head, dkey_head, dvalue_head = operands
    score_scale = 1.0 / jnp.sqrt(jnp.float32(HEAD_DIM))
    scores = jnp.dot(query_head, key_head.T, preferred_element_type=jnp.float32) * score_scale
    d_scores = (jnp.dot(dquery_head, key_head.T, preferred_element_type=jnp.float32) + jnp.dot(query_head, dkey_head.T, preferred_element_type=jnp.float32)) * score_scale
    row_peak = lax.optimization_barrier(jnp.max(scores, axis=1, keepdims=True))
    weights = jnp.exp(scores - row_peak)
    row_total = lax.optimization_barrier(jnp.sum(weights, axis=1))
    mixed = weights * d_scores
    row_slope = lax.optimization_barrier(jnp.sum(mixed, axis=1))
    weights_low = weights.astype(jnp.bfloat16)
    mixed_low = mixed.astype(jnp.bfloat16)
    accum = jnp.dot(weights_low, value_head, preferred_element_type=jnp.float32)
    tangent = jnp.dot(mixed_low, value_head, preferred_element_type=jnp.float32) + jnp.dot(weights_low, dvalue_head, preferred_element_type=jnp.float32)
    attended = accum / row_total[:, None]
    d_attended = tangent / row_total[:, None] - (row_slope / row_total)[:, None] * attended
    return (attended, d_attended)

def split_heads(array):
    return array.reshape(LENGTH, HEADS, HEAD_DIM).transpose(1, 0, 2)

def reference(query, key, value, d_query, d_key, d_value, residual, d_residual, w_in, w_out):
    operands = tuple((split_heads(array) for array in (query, key, value, d_query, d_key, d_value)))
    attended, d_attended = lax.map(head_attend, operands)
    attended = attended.transpose(1, 0, 2).reshape(LENGTH, D)
    d_attended = d_attended.transpose(1, 0, 2).reshape(LENGTH, D)
    mixed_in = (residual.astype(jnp.float32) + attended).astype(jnp.bfloat16)
    d_mixed_in = (d_residual.astype(jnp.float32) + d_attended).astype(jnp.bfloat16)
    pre_act = jnp.dot(mixed_in, w_in, preferred_element_type=jnp.float32)
    d_pre_act = jnp.dot(d_mixed_in, w_in, preferred_element_type=jnp.float32)
    hidden, d_hidden = gelu_pair(pre_act, d_pre_act)
    hidden = hidden.astype(jnp.bfloat16)
    d_hidden = d_hidden.astype(jnp.bfloat16)
    block_out = (mixed_in.astype(jnp.float32) + jnp.dot(hidden, w_out, preferred_element_type=jnp.float32)).astype(jnp.bfloat16)
    d_block_out = (d_mixed_in.astype(jnp.float32) + jnp.dot(d_hidden, w_out, preferred_element_type=jnp.float32)).astype(jnp.bfloat16)
    return (block_out, d_block_out)
```

```python
import functools
import math

import jax
import jax.numpy as jnp
from jax import lax
from jax.experimental import pallas as pl
from jax.experimental.pallas import tpu as pltpu
from jax.sharding import PartitionSpec as P

HEAD_DIM = 128


gelu_coeff = 0.7978845608
cubic_coeff = 0.044715


def gelu_pair(pre_act, d_pre_act):
    inner_arg = gelu_coeff * (pre_act + cubic_coeff * pre_act * pre_act * pre_act)
    hyper = jnp.tanh(inner_arg)
    gelu_value = 0.5 * pre_act * (1.0 + hyper)
    gelu_slope = 0.5 * (1.0 + hyper) + 0.5 * pre_act * (1.0 - hyper * hyper) * gelu_coeff * (
        1.0 + 3.0 * cubic_coeff * pre_act * pre_act
    )
    return (gelu_value, gelu_slope * d_pre_act)


def nt(a, b):
    return lax.dot_general(a, b, (((1,), (1,)), ((), ())), preferred_element_type=jnp.float32)


def attend_kernel(q, dq, res, dres, k, v, dk, dv, out, *, rows):
    scale = 1.0 / math.sqrt(HEAD_DIM)
    keys = k[...]
    keys_pair = jnp.concatenate([keys, dk[...]], axis=1)
    values = v[...]
    values_pair = jnp.concatenate([values, dv[...]], axis=1)
    for start in range(0, q.shape[0], rows):
        part = pl.ds(start, rows)
        scores = nt(q[part, :], keys) * scale
        d_scores = nt(jnp.concatenate([dq[part, :], q[part, :]], axis=1), keys_pair) * scale
        peak = jnp.max(scores, axis=1, keepdims=True)
        weights = jnp.exp(scores - peak)
        mixed = weights * d_scores
        total = jnp.sum(weights, axis=1, keepdims=True)
        slope = jnp.sum(mixed, axis=1, keepdims=True)
        both = jnp.dot(
            weights.astype(jnp.bfloat16), values_pair, preferred_element_type=jnp.float32
        )
        tangent = both[:, HEAD_DIM:] + jnp.dot(
            mixed.astype(jnp.bfloat16), values, preferred_element_type=jnp.float32
        )
        attended = both[:, :HEAD_DIM] / total
        d_attended = tangent / total - (slope / total) * attended
        out[0, part, :] = (res[part, :].astype(jnp.float32) + attended).astype(jnp.bfloat16)
        out[1, part, :] = (dres[part, :].astype(jnp.float32) + d_attended).astype(jnp.bfloat16)


def attend(query, d_query, residual, d_residual, kv):
    rows, feats = query.shape
    heads = feats // HEAD_DIM
    length = kv.shape[0]
    own = pl.BlockSpec((rows, HEAD_DIM), lambda h: (0, h))

    def kv_spec(i):
        return pl.BlockSpec((length, HEAD_DIM), lambda h: (0, i * heads + h))

    return pl.pallas_call(
        functools.partial(attend_kernel, rows=min(rows, 128)),
        grid=(heads,),
        in_specs=[own] * 4 + [kv_spec(i) for i in range(4)],
        out_specs=pl.BlockSpec((2, rows, HEAD_DIM), lambda h: (0, 0, h)),
        out_shape=jax.ShapeDtypeStruct((2, rows, feats), jnp.bfloat16),
        cost_estimate=pl.CostEstimate(
            flops=12 * rows * length * feats, bytes_accessed=8 * length * feats, transcendentals=0
        ),
        name="attend",
    )(query, d_query, residual, d_residual, kv, kv, kv, kv)


def on_device(query, key, value, d_query, d_key, d_value, residual, d_residual, w_in, w_out):
    rows, feats = query.shape
    kv = lax.all_gather(
        jnp.concatenate([key, value, d_key, d_value], axis=1), "seq", axis=0, tiled=True
    )
    w_in_whole = lax.all_gather(w_in, "seq", axis=0, tiled=True)
    w_out_whole = lax.all_gather(w_out, "seq", axis=0, tiled=True)
    mixed = attend(query, d_query, residual, d_residual, kv).reshape(2 * rows, feats)
    whole = lax.all_gather(mixed, "dp", axis=1, tiled=True)
    pre = jnp.dot(whole, w_in_whole, preferred_element_type=jnp.float32)
    hidden, d_hidden = gelu_pair(pre[:rows], pre[rows:])
    hidden = jnp.concatenate([hidden.astype(jnp.bfloat16), d_hidden.astype(jnp.bfloat16)], axis=0)
    partial = jnp.dot(hidden, w_out_whole, preferred_element_type=jnp.float32)
    summed = lax.psum_scatter(
        partial.astype(jnp.bfloat16), "dp", scatter_dimension=1, tiled=True
    ).astype(jnp.float32)
    out = (mixed.astype(jnp.float32) + summed).astype(jnp.bfloat16)
    return (out[:rows], out[rows:])


def solution(mesh):
    in_specs = (P("seq", "dp"),) * 9 + (P(("dp", "seq"), None),)
    out_specs = (P("seq", "dp"), P("seq", "dp"))
    return jax.shard_map(
        on_device, mesh=mesh, in_specs=in_specs, out_specs=out_specs, check_vma=False
    )
```

```python
import functools
import math

import jax
import jax.numpy as jnp
from jax import lax
from jax.experimental import pallas as pl
from jax.experimental.pallas import tpu as pltpu
from jax.sharding import PartitionSpec as P

HEAD_DIM = 128


gelu_coeff = 0.7978845608
cubic_coeff = 0.044715


def gelu_pair(pre_act, d_pre_act):
    inner_arg = gelu_coeff * (pre_act + cubic_coeff * pre_act * pre_act * pre_act)
    hyper = jnp.tanh(inner_arg)
    gelu_value = 0.5 * pre_act * (1.0 + hyper)
    gelu_slope = 0.5 * (1.0 + hyper) + 0.5 * pre_act * (1.0 - hyper * hyper) * gelu_coeff * (
        1.0 + 3.0 * cubic_coeff * pre_act * pre_act
    )
    return (gelu_value, gelu_slope * d_pre_act)


def nt(a, b):
    return lax.dot_general(a, b, (((1,), (1,)), ((), ())), preferred_element_type=jnp.float32)


def attend_math(q, dq, res, dres, keys, values, keys_pair, values_pair):
    scale = 1.0 / math.sqrt(HEAD_DIM)
    scores = nt(q, keys) * scale
    d_scores = nt(jnp.concatenate([dq, q], axis=1), keys_pair) * scale
    peak = jnp.max(scores, axis=1, keepdims=True)
    weights = jnp.exp(scores - peak)
    mixed = weights * d_scores
    total = jnp.sum(weights, axis=1, keepdims=True)
    slope = jnp.sum(mixed, axis=1, keepdims=True)
    both = jnp.dot(weights.astype(jnp.bfloat16), values_pair, preferred_element_type=jnp.float32)
    tangent = both[:, HEAD_DIM:] + jnp.dot(
        mixed.astype(jnp.bfloat16), values, preferred_element_type=jnp.float32
    )
    attended = both[:, :HEAD_DIM] / total
    d_attended = tangent / total - (slope / total) * attended
    return (
        (res.astype(jnp.float32) + attended).astype(jnp.bfloat16),
        (dres.astype(jnp.float32) + d_attended).astype(jnp.bfloat16),
    )


def attend_kernel(q, dq, res, dres, k, v, dk, dv, out, *, rows):
    keys, values = k[...], v[...]
    keys_pair = jnp.concatenate([keys, dk[...]], axis=1)
    values_pair = jnp.concatenate([values, dv[...]], axis=1)
    for start in range(0, q.shape[0], rows):
        part = pl.ds(start, rows)
        out[0, part, :], out[1, part, :] = attend_math(
            q[part, :], dq[part, :], res[part, :], dres[part, :],
            keys, values, keys_pair, values_pair,
        )


def attend(query, d_query, residual, d_residual, kv):
    rows, feats = query.shape
    heads = feats // HEAD_DIM
    length = kv.shape[0]
    own = pl.BlockSpec((rows, HEAD_DIM), lambda h: (0, h))

    def kv_spec(i):
        return pl.BlockSpec((length, HEAD_DIM), lambda h: (0, i * heads + h))

    return pl.pallas_call(
        functools.partial(attend_kernel, rows=min(rows, 128)),
        grid=(heads,),
        in_specs=[own] * 4 + [kv_spec(i) for i in range(4)],
        out_specs=pl.BlockSpec((2, rows, HEAD_DIM), lambda h: (0, 0, h)),
        out_shape=jax.ShapeDtypeStruct((2, rows, feats), jnp.bfloat16),
        cost_estimate=pl.CostEstimate(
            flops=12 * rows * length * feats, bytes_accessed=8 * length * feats, transcendentals=0
        ),
        name="attend",
    )(query, d_query, residual, d_residual, kv, kv, kv, kv)


def by_rows(query, key, value, d_query, d_key, d_value, residual, d_residual, w_in, w_out):
    rows, feats = query.shape
    kv = lax.all_gather(
        jnp.concatenate([key, value, d_key, d_value], axis=1), "seq", axis=0, tiled=True
    )
    w_in_whole = lax.all_gather(w_in, "seq", axis=0, tiled=True)
    w_out_whole = lax.all_gather(w_out, "seq", axis=0, tiled=True)
    mixed = attend(query, d_query, residual, d_residual, kv).reshape(2 * rows, feats)
    whole = lax.all_gather(mixed, "dp", axis=1, tiled=True)
    pre = jnp.dot(whole, w_in_whole, preferred_element_type=jnp.float32)
    hidden, d_hidden = gelu_pair(pre[:rows], pre[rows:])
    hidden = jnp.concatenate([hidden.astype(jnp.bfloat16), d_hidden.astype(jnp.bfloat16)], axis=0)
    partial = jnp.dot(hidden, w_out_whole, preferred_element_type=jnp.float32)
    summed = lax.psum_scatter(
        partial.astype(jnp.bfloat16), "dp", scatter_dimension=1, tiled=True
    ).astype(jnp.float32)
    out = (mixed.astype(jnp.float32) + summed).astype(jnp.bfloat16)
    return (out[:rows], out[rows:])


INNER = 4
MESH = pl.DeviceIdType.MESH


def place(groups):
    seq = lax.axis_index("seq")
    return lax.axis_index("dp"), lax.div(seq, INNER), lax.rem(seq, INNER)


def enter(devices):
    barrier = pltpu.get_barrier_semaphore()
    for device in devices:
        pl.semaphore_signal(barrier, inc=1, device_id=device, device_id_type=MESH)
    pl.semaphore_wait(barrier, len(devices))


def spread_kernel(
    q, dq, res, dres, k, v, dk, dv, w_in, own, kv, win, z_send, z_recv, own_sem,
    p_send, p_recv, y_send, y_recv, f_send, f_recv,
):
    groups, width = own.shape[1], own.shape[3]
    hid = win.shape[2]
    x, g, i = place(groups)
    partner = (x, g * INNER + i + 1 - 2 * lax.rem(i, 2))
    across_i = lax.rem(i + 2, INNER)
    across = (x, g * INNER + across_i)
    peers = [(x, lax.rem(g + t, groups) * INNER + i) for t in range(1, groups)]
    enter(peers + [partner, across])

    def piece(j, to):
        if j < 4:
            return (k, v, dk, dv)[j].at[:, pl.ds(pl.multiple_of(to * width, 128), width)]
        if j < 8:
            return (q, dq, res, dres)[j - 4].at[:, pl.ds(pl.multiple_of(to * width, 128), width)]
        return w_in.at[:, pl.ds(pl.multiple_of(to * hid, 128), hid)]

    def slot(j, source):
        if j < 4:
            return kv.at[i, source, j]
        if j < 8:
            return own.at[j - 4, source]
        return win.at[source]

    def over_z(t, j):
        return pltpu.make_async_remote_copy(
            src_ref=piece(j, lax.rem(g + t, groups)),
            dst_ref=slot(j, g),
            send_sem=z_send.at[t - 1, j],
            recv_sem=z_recv.at[t - 1, j],
            device_id=peers[t - 1],
            device_id_type=MESH,
        )

    def layer(block, source, send, recv, t, device):
        return pltpu.make_async_remote_copy(
            src_ref=kv.at[block, source],
            dst_ref=kv.at[block, source],
            send_sem=send.at[t],
            recv_sem=recv.at[t],
            device_id=device,
            device_id_type=MESH,
        )

    z_copies = {}
    for order in (range(8), (8,)):
        for t in range(1, groups):
            for j in order:
                z_copies[t, j] = over_z(t, j)
                z_copies[t, j].start()
    locals_ = [pltpu.make_async_copy(piece(j, g), slot(j, g), own_sem.at[j]) for j in range(9)]
    for copy in locals_:
        copy.start()
    for copy in locals_:
        copy.wait()
    inside, forwards = [], []

    def forward(t):
        inside[t][1].wait_recv()
        source = lax.rem(g + groups - t, groups)
        copy = layer(across_i, source, f_send, f_recv, t, partner)
        copy.start()
        forwards.append(copy)

    for t in range(groups):
        if t:
            for j in range(4):
                z_copies[t, j].wait_recv()
        source = lax.rem(g + groups - t, groups)
        pair = (
            layer(i, source, p_send, p_recv, t, partner),
            layer(i, source, y_send, y_recv, t, across),
        )
        pair[1].start()
        pair[0].start()
        inside.append(pair)
        if t:
            forward(t - 1)
    forward(groups - 1)
    for t in range(groups):
        inside[t][0].wait()
        inside[t][1].wait_send()
        forwards[t].wait()
    for (t, j), copy in z_copies.items():
        copy.wait_send()
        if j >= 4:
            copy.wait_recv()


def spread(tensors, w_in, groups):
    rows, feats = tensors[0].shape
    width = feats // groups
    deep, hid = w_in.shape[0], w_in.shape[1] // groups
    dma = pltpu.SemaphoreType.DMA
    return pl.pallas_call(
        spread_kernel,
        in_specs=[pl.BlockSpec(memory_space=pltpu.VMEM)] * 9,
        out_specs=[pl.BlockSpec(memory_space=pl.ANY)] * 3,
        out_shape=[
            jax.ShapeDtypeStruct((4, groups, rows, width), jnp.bfloat16),
            jax.ShapeDtypeStruct((INNER, groups, 4, rows, width), jnp.bfloat16),
            jax.ShapeDtypeStruct((groups, deep, hid), jnp.bfloat16),
        ],
        scratch_shapes=[dma((groups - 1, 9)), dma((groups - 1, 9)), dma((9,))]
        + [dma((groups,)) for _ in range(6)],
        compiler_params=pltpu.CompilerParams(collective_id=0, has_side_effects=True),
        name="spread",
    )(*tensors, w_in)


def attend_wide_kernel(q, dq, res, dres, k, v, dk, dv, out):
    length = k.shape[0] * k.shape[1] * k.shape[3]
    keys, values, d_keys, d_values = (
        ref[...].reshape(length, HEAD_DIM) for ref in (k, v, dk, dv)
    )
    keys_pair = jnp.concatenate([keys, d_keys], axis=1)
    values_pair = jnp.concatenate([values, d_values], axis=1)
    half = out.shape[3]
    for g in range(q.shape[1]):
        pair = attend_math(
            q[0, g], dq[0, g], res[0, g], dres[0, g], keys, values, keys_pair, values_pair
        )
        for side in range(out.shape[0]):
            for kind in range(2):
                out[side, kind, g] = pair[kind][side * half : (side + 1) * half]


def attend_wide(own, kv, sides):
    _, groups, rows, width = own.shape
    heads = width // HEAD_DIM
    half = rows // sides

    def own_spec(i):
        return pl.BlockSpec((1, groups, rows, HEAD_DIM), lambda h: (i, 0, 0, h))

    def kv_spec(i):
        return pl.BlockSpec((INNER, groups, 1, rows, HEAD_DIM), lambda h: (0, 0, i, 0, h))

    return pl.pallas_call(
        attend_wide_kernel,
        grid=(heads,),
        in_specs=[own_spec(i) for i in range(4)] + [kv_spec(i) for i in range(4)],
        out_specs=pl.BlockSpec((sides, 2, groups, half, HEAD_DIM), lambda h: (0, 0, 0, 0, h)),
        out_shape=jax.ShapeDtypeStruct((sides, 2, groups, half, width), jnp.bfloat16),
        cost_estimate=pl.CostEstimate(
            flops=12 * INNER * (groups * rows) ** 2 * width,
            bytes_accessed=8 * INNER * groups * rows * width,
            transcendentals=0,
        ),
        name="attend_wide",
    )(own, own, own, own, kv, kv, kv, kv)


def line_kernel(block, out, own_sem, right_send, right_recv, left_send, left_recv):
    groups = out.shape[0]
    x, g, i = place(groups)
    last = groups - 1
    right = (x, jnp.minimum(g + 1, last) * INNER + i)
    left = (x, jnp.maximum(g - 1, 0) * INNER + i)
    enter([(x, lax.rem(g + t, groups) * INNER + i) for t in range(1, groups)])

    def hop(t, first, to_right):
        source = g - t if to_right else g + t
        sends, recvs = (right_send, right_recv) if to_right else (left_send, left_recv)
        return pltpu.make_async_remote_copy(
            src_ref=block if first else out.at[source],
            dst_ref=out.at[source],
            send_sem=sends.at[t],
            recv_sem=recvs.at[t],
            device_id=right if to_right else left,
            device_id_type=MESH,
        )

    mine = pltpu.make_async_copy(block, out.at[g], own_sem)
    mine.start()
    for t in range(last):
        if t:

            @pl.when(g >= t)
            def _():
                hop(t - 1, False, True).wait_recv()

        @pl.when((g >= t) & (g < last))
        def _():
            hop(t, t == 0, True).start()

        if t:

            @pl.when(g + t <= last)
            def _():
                hop(t - 1, False, False).wait_recv()

        @pl.when((g + t <= last) & (g > 0))
        def _():
            hop(t, t == 0, False).start()

    @pl.when(g >= last)
    def _():
        hop(last - 1, False, True).wait_recv()

    @pl.when(g + last <= last)
    def _():
        hop(last - 1, False, False).wait_recv()

    for t in range(last):

        @pl.when((g >= t) & (g < last))
        def _():
            hop(t, t == 0, True).wait_send()

        @pl.when((g + t <= last) & (g > 0))
        def _():
            hop(t, t == 0, False).wait_send()

    mine.wait()


def along_line(block, groups):
    dma = pltpu.SemaphoreType.DMA
    return pl.pallas_call(
        line_kernel,
        in_specs=[pl.BlockSpec(memory_space=pltpu.VMEM)],
        out_specs=pl.BlockSpec(memory_space=pl.ANY),
        out_shape=jax.ShapeDtypeStruct((groups,) + block.shape, block.dtype),
        scratch_shapes=[dma] + [dma((groups - 1,)) for _ in range(4)],
        compiler_params=pltpu.CompilerParams(collective_id=1, has_side_effects=True),
        name="along_line",
    )(block)


def return_kernel(partial, out, own_sem, send, recv):
    groups = out.shape[0]
    x, g, i = place(groups)
    peers = [(x, lax.rem(g + t, groups) * INNER + i) for t in range(1, groups)]
    enter(peers)
    copies = [
        pltpu.make_async_remote_copy(
            src_ref=partial.at[lax.rem(g + t, groups)],
            dst_ref=out.at[t],
            send_sem=send.at[t - 1],
            recv_sem=recv.at[t - 1],
            device_id=peers[t - 1],
            device_id_type=MESH,
        )
        for t in range(1, groups)
    ]
    for copy in copies:
        copy.start()
    mine = pltpu.make_async_copy(partial.at[g], out.at[0], own_sem)
    mine.start()
    mine.wait()
    for copy in copies:
        copy.wait()


def send_back(partial):
    groups = partial.shape[0]
    dma = pltpu.SemaphoreType.DMA
    return pl.pallas_call(
        return_kernel,
        in_specs=[pl.BlockSpec(memory_space=pltpu.VMEM)],
        out_specs=pl.BlockSpec(memory_space=pl.ANY),
        out_shape=jax.ShapeDtypeStruct(partial.shape, partial.dtype),
        scratch_shapes=[dma, dma((groups - 1,)), dma((groups - 1,))],
        compiler_params=pltpu.CompilerParams(collective_id=2, has_side_effects=True),
        name="send_back",
    )(partial)


def hidden_kernel(a, w, out, total):
    step = pl.program_id(1)
    left = jnp.concatenate([a[j, 0] for j in range(a.shape[0])], axis=1)
    depth, hid = left.shape[1], w.shape[4]
    product = jnp.dot(left, w[...].reshape(depth, hid), preferred_element_type=jnp.float32)

    @pl.when(step == 0)
    def _():
        total[...] = product

    @pl.when(step > 0)
    def _():
        total[...] += product

    @pl.when(step == pl.num_programs(1) - 1)
    def _():
        rows = total.shape[0] // 2
        value, tangent = gelu_pair(total[:rows], total[rows:])
        out[:rows] = value.astype(jnp.bfloat16)
        out[rows:] = tangent.astype(jnp.bfloat16)


def hidden_layer(gathered, w, dp):
    groups, _, rows, width = gathered.shape
    deep, hid = w.shape[3:]
    per = groups // dp
    return pl.pallas_call(
        hidden_kernel,
        grid=(dp, groups),
        in_specs=[
            pl.BlockSpec((dp, 1, rows, width), lambda f, k: (lax.rem(k, per), lax.div(k, per), 0, 0)),
            pl.BlockSpec((1, INNER, 1, deep, hid), lambda f, k: (f, 0, k, 0, 0)),
        ],
        out_specs=pl.BlockSpec((rows, hid), lambda f, k: (0, f)),
        out_shape=jax.ShapeDtypeStruct((rows, dp * hid), jnp.bfloat16),
        scratch_shapes=[pltpu.VMEM((rows, hid), jnp.float32)],
        cost_estimate=pl.CostEstimate(
            flops=2 * rows * groups * dp * width * dp * hid,
            bytes_accessed=2 * dp * INNER * groups * deep * hid,
            transcendentals=0,
        ),
        name="hidden_layer",
    )(gathered, w)


def in_layer(block, dp, seq):
    layers = [
        [d * seq + layer * INNER + i for d in range(dp) for i in range(INNER)]
        for layer in range(seq // INNER)
    ]
    return lax.all_gather(block, ("dp", "seq"), axis_index_groups=layers, axis=0, tiled=False)


def by_layers(query, key, value, d_query, d_key, d_value, residual, d_residual, w_in, w_out, dp, seq):
    groups = seq // INNER
    rows, feats = query.shape
    half, width = rows // dp, feats // groups
    w_out_layer = in_layer(w_out, dp, seq).reshape(dp * INNER * w_out.shape[0], w_out.shape[1])
    own, kv, win = spread(
        (query, d_query, residual, d_residual, key, value, d_key, d_value), w_in, groups
    )
    w_in_layer = in_layer(win, dp, seq).reshape((dp, INNER) + win.shape)
    mixed = attend_wide(own, kv, dp)
    block = lax.all_to_all(mixed, "dp", split_axis=0, concat_axis=0, tiled=True)
    gathered = along_line(block, groups)
    hidden = hidden_layer(gathered.reshape(groups, dp, 2 * groups * half, width), w_in_layer, dp)
    partial = jnp.dot(hidden, w_out_layer, preferred_element_type=jnp.float32).astype(jnp.bfloat16)
    partial = partial.reshape(2, groups, half, dp * feats).transpose(1, 0, 2, 3)
    sums = jnp.sum(send_back(partial).astype(jnp.float32), axis=0)
    g = lax.div(lax.axis_index("seq"), INNER)
    base = lax.dynamic_index_in_dim(gathered, g, axis=3, keepdims=False)
    base = base.transpose(2, 3, 1, 0, 4).reshape(2, half, dp * feats)
    done = (base.astype(jnp.float32) + sums).astype(jnp.bfloat16)
    out = lax.all_to_all(done, "dp", split_axis=2, concat_axis=1, tiled=True)
    return (out[0], out[1])


def on_device(*args, dp, seq):
    query, w_in = args[0], args[8]
    groups = seq // INNER
    tile = groups * HEAD_DIM
    if seq % INNER or groups < 2 or groups % dp or query.shape[1] % tile or w_in.shape[1] % tile:
        return by_rows(*args)
    return by_layers(*args, dp=dp, seq=seq)


def solution(mesh):
    in_specs = (P("seq", "dp"),) * 9 + (P(("dp", "seq"), None),)
    out_specs = (P("seq", "dp"), P("seq", "dp"))
    body = functools.partial(on_device, dp=mesh.shape["dp"], seq=mesh.shape["seq"])
    return jax.shard_map(
        body, mesh=mesh, in_specs=in_specs, out_specs=out_specs, check_vma=False
    )
```

```python
import functools
import math

import jax
import jax.numpy as jnp
from jax import lax
from jax.experimental import pallas as pl
from jax.experimental.pallas import tpu as pltpu
from jax.sharding import PartitionSpec as P

HEAD_DIM = 128


gelu_coeff = 0.7978845608
cubic_coeff = 0.044715


def gelu_pair(pre_act, d_pre_act):
    inner_arg = gelu_coeff * (pre_act + cubic_coeff * pre_act * pre_act * pre_act)
    hyper = jnp.tanh(inner_arg)
    gelu_value = 0.5 * pre_act * (1.0 + hyper)
    gelu_slope = 0.5 * (1.0 + hyper) + 0.5 * pre_act * (1.0 - hyper * hyper) * gelu_coeff * (
        1.0 + 3.0 * cubic_coeff * pre_act * pre_act
    )
    return (gelu_value, gelu_slope * d_pre_act)


def nt(a, b):
    return lax.dot_general(a, b, (((1,), (1,)), ((), ())), preferred_element_type=jnp.float32)


def attend_math(q, dq, res, dres, keys, values, keys_pair, values_pair):
    scale = 1.0 / math.sqrt(HEAD_DIM)
    scores = nt(q, keys) * scale
    d_scores = nt(jnp.concatenate([dq, q], axis=1), keys_pair) * scale
    peak = jnp.max(scores, axis=1, keepdims=True)
    weights = jnp.exp(scores - peak)
    mixed = weights * d_scores
    total = jnp.sum(weights, axis=1, keepdims=True)
    slope = jnp.sum(mixed, axis=1, keepdims=True)
    both = jnp.dot(weights.astype(jnp.bfloat16), values_pair, preferred_element_type=jnp.float32)
    tangent = both[:, HEAD_DIM:] + jnp.dot(
        mixed.astype(jnp.bfloat16), values, preferred_element_type=jnp.float32
    )
    attended = both[:, :HEAD_DIM] / total
    d_attended = tangent / total - (slope / total) * attended
    return (
        (res.astype(jnp.float32) + attended).astype(jnp.bfloat16),
        (dres.astype(jnp.float32) + d_attended).astype(jnp.bfloat16),
    )


def attend_kernel(q, dq, res, dres, k, v, dk, dv, out, *, rows):
    keys, values = k[...], v[...]
    keys_pair = jnp.concatenate([keys, dk[...]], axis=1)
    values_pair = jnp.concatenate([values, dv[...]], axis=1)
    for start in range(0, q.shape[0], rows):
        part = pl.ds(start, rows)
        out[0, part, :], out[1, part, :] = attend_math(
            q[part, :], dq[part, :], res[part, :], dres[part, :],
            keys, values, keys_pair, values_pair,
        )


def attend(query, d_query, residual, d_residual, kv):
    rows, feats = query.shape
    heads = feats // HEAD_DIM
    length = kv.shape[0]
    own = pl.BlockSpec((rows, HEAD_DIM), lambda h: (0, h))

    def kv_spec(i):
        return pl.BlockSpec((length, HEAD_DIM), lambda h: (0, i * heads + h))

    return pl.pallas_call(
        functools.partial(attend_kernel, rows=min(rows, 128)),
        grid=(heads,),
        in_specs=[own] * 4 + [kv_spec(i) for i in range(4)],
        out_specs=pl.BlockSpec((2, rows, HEAD_DIM), lambda h: (0, 0, h)),
        out_shape=jax.ShapeDtypeStruct((2, rows, feats), jnp.bfloat16),
        cost_estimate=pl.CostEstimate(
            flops=12 * rows * length * feats, bytes_accessed=8 * length * feats, transcendentals=0
        ),
        name="attend",
    )(query, d_query, residual, d_residual, kv, kv, kv, kv)


def by_rows(query, key, value, d_query, d_key, d_value, residual, d_residual, w_in, w_out):
    rows, feats = query.shape
    kv = lax.all_gather(
        jnp.concatenate([key, value, d_key, d_value], axis=1), "seq", axis=0, tiled=True
    )
    w_in_whole = lax.all_gather(w_in, "seq", axis=0, tiled=True)
    w_out_whole = lax.all_gather(w_out, "seq", axis=0, tiled=True)
    mixed = attend(query, d_query, residual, d_residual, kv).reshape(2 * rows, feats)
    whole = lax.all_gather(mixed, "dp", axis=1, tiled=True)
    pre = jnp.dot(whole, w_in_whole, preferred_element_type=jnp.float32)
    hidden, d_hidden = gelu_pair(pre[:rows], pre[rows:])
    hidden = jnp.concatenate([hidden.astype(jnp.bfloat16), d_hidden.astype(jnp.bfloat16)], axis=0)
    partial = jnp.dot(hidden, w_out_whole, preferred_element_type=jnp.float32)
    summed = lax.psum_scatter(
        partial.astype(jnp.bfloat16), "dp", scatter_dimension=1, tiled=True
    ).astype(jnp.float32)
    out = (mixed.astype(jnp.float32) + summed).astype(jnp.bfloat16)
    return (out[:rows], out[rows:])


INNER = 4
MESH = pl.DeviceIdType.MESH
COMM_COST = pl.CostEstimate(flops=10**11, bytes_accessed=10**8, transcendentals=0)


def place(groups):
    seq = lax.axis_index("seq")
    return lax.axis_index("dp"), lax.div(seq, INNER), lax.rem(seq, INNER)


def enter(devices):
    barrier = pltpu.get_barrier_semaphore()
    for device in devices:
        pl.semaphore_signal(barrier, inc=1, device_id=device, device_id_type=MESH)
    pl.semaphore_wait(barrier, len(devices))


def spread_kernel(
    q, dq, res, dres, k, v, dk, dv, w_in, own, kv, win, z_send, z_recv, own_sem,
    p_send, p_recv, y_send, y_recv, f_send, f_recv,
):
    groups, width = own.shape[1], own.shape[3]
    hid = win.shape[2]
    x, g, i = place(groups)
    partner = (x, g * INNER + i + 1 - 2 * lax.rem(i, 2))
    across_i = lax.rem(i + 2, INNER)
    across = (x, g * INNER + across_i)
    peers = [(x, lax.rem(g + t, groups) * INNER + i) for t in range(1, groups)]
    enter(peers + [partner, across])

    def piece(j, to):
        if j < 4:
            return (k, v, dk, dv)[j].at[:, pl.ds(pl.multiple_of(to * width, 128), width)]
        if j < 8:
            return (q, dq, res, dres)[j - 4].at[:, pl.ds(pl.multiple_of(to * width, 128), width)]
        return w_in.at[:, pl.ds(pl.multiple_of(to * hid, 128), hid)]

    def slot(j, source):
        if j < 4:
            return kv.at[i, source, j]
        if j < 8:
            return own.at[j - 4, source]
        return win.at[source]

    def over_z(t, j):
        return pltpu.make_async_remote_copy(
            src_ref=piece(j, lax.rem(g + t, groups)),
            dst_ref=slot(j, g),
            send_sem=z_send.at[t - 1, j],
            recv_sem=z_recv.at[t - 1, j],
            device_id=peers[t - 1],
            device_id_type=MESH,
        )

    def layer(block, source, send, recv, t, device):
        return pltpu.make_async_remote_copy(
            src_ref=kv.at[block, source],
            dst_ref=kv.at[block, source],
            send_sem=send.at[t],
            recv_sem=recv.at[t],
            device_id=device,
            device_id_type=MESH,
        )

    z_copies = {}
    for order in (range(8), (8,)):
        for t in range(1, groups):
            for j in order:
                z_copies[t, j] = over_z(t, j)
                z_copies[t, j].start()
    locals_ = [pltpu.make_async_copy(piece(j, g), slot(j, g), own_sem.at[j]) for j in range(9)]
    for copy in locals_:
        copy.start()
    for copy in locals_:
        copy.wait()
    inside, forwards = [], []

    def forward(t):
        inside[t][1].wait_recv()
        source = lax.rem(g + groups - t, groups)
        copy = layer(across_i, source, f_send, f_recv, t, partner)
        copy.start()
        forwards.append(copy)

    for t in range(groups):
        if t:
            for j in range(4):
                z_copies[t, j].wait_recv()
        source = lax.rem(g + groups - t, groups)
        pair = (
            layer(i, source, p_send, p_recv, t, partner),
            layer(i, source, y_send, y_recv, t, across),
        )
        pair[1].start()
        pair[0].start()
        inside.append(pair)
        if t:
            forward(t - 1)
    forward(groups - 1)
    for t in range(groups):
        inside[t][0].wait()
        inside[t][1].wait_send()
        forwards[t].wait()
    for (t, j), copy in z_copies.items():
        copy.wait_send()
        if j >= 4:
            copy.wait_recv()


def spread(tensors, w_in, groups):
    rows, feats = tensors[0].shape
    width = feats // groups
    deep, hid = w_in.shape[0], w_in.shape[1] // groups
    dma = pltpu.SemaphoreType.DMA
    return pl.pallas_call(
        spread_kernel,
        in_specs=[pl.BlockSpec(memory_space=pltpu.VMEM)] * 9,
        out_specs=[pl.BlockSpec(memory_space=pl.ANY)] * 3,
        out_shape=[
            jax.ShapeDtypeStruct((4, groups, rows, width), jnp.bfloat16),
            jax.ShapeDtypeStruct((INNER, groups, 4, rows, width), jnp.bfloat16),
            jax.ShapeDtypeStruct((groups, deep, hid), jnp.bfloat16),
        ],
        scratch_shapes=[dma((groups - 1, 9)), dma((groups - 1, 9)), dma((9,))]
        + [dma((groups,)) for _ in range(6)],
        cost_estimate=COMM_COST,
        compiler_params=pltpu.CompilerParams(collective_id=0, has_side_effects=True),
        name="spread",
    )(*tensors, w_in)


def attend_wide_kernel(q, dq, res, dres, k, v, dk, dv, out):
    length = k.shape[0] * k.shape[1] * k.shape[3]
    keys, values, d_keys, d_values = (
        ref[...].reshape(length, HEAD_DIM) for ref in (k, v, dk, dv)
    )
    keys_pair = jnp.concatenate([keys, d_keys], axis=1)
    values_pair = jnp.concatenate([values, d_values], axis=1)
    half = out.shape[3]
    for g in range(q.shape[1]):
        pair = attend_math(
            q[0, g], dq[0, g], res[0, g], dres[0, g], keys, values, keys_pair, values_pair
        )
        for side in range(out.shape[0]):
            for kind in range(2):
                out[side, kind, g] = pair[kind][side * half : (side + 1) * half]


def attend_wide(own, kv, sides):
    _, groups, rows, width = own.shape
    heads = width // HEAD_DIM
    half = rows // sides

    def own_spec(i):
        return pl.BlockSpec((1, groups, rows, HEAD_DIM), lambda h: (i, 0, 0, h))

    def kv_spec(i):
        return pl.BlockSpec((INNER, groups, 1, rows, HEAD_DIM), lambda h: (0, 0, i, 0, h))

    return pl.pallas_call(
        attend_wide_kernel,
        grid=(heads,),
        in_specs=[own_spec(i) for i in range(4)] + [kv_spec(i) for i in range(4)],
        out_specs=pl.BlockSpec((sides, 2, groups, half, HEAD_DIM), lambda h: (0, 0, 0, 0, h)),
        out_shape=jax.ShapeDtypeStruct((sides, 2, groups, half, width), jnp.bfloat16),
        cost_estimate=pl.CostEstimate(
            flops=12 * INNER * (groups * rows) ** 2 * width,
            bytes_accessed=8 * INNER * groups * rows * width,
            transcendentals=0,
        ),
        name="attend_wide",
    )(own, own, own, own, kv, kv, kv, kv)


def line_kernel(
    mixed, out, own_sem, x_send, x_recv, right_send, right_recv, left_send, left_recv
):
    groups = out.shape[0]
    x, g, i = place(groups)
    last = groups - 1
    other = 1 - x
    right = (x, jnp.minimum(g + 1, last) * INNER + i)
    left = (x, jnp.maximum(g - 1, 0) * INNER + i)
    twin = (other, g * INNER + i)
    enter([(x, lax.rem(g + t, groups) * INNER + i) for t in range(1, groups)] + [twin])

    def hop(c, t, to_right):
        source = g - t if to_right else g + t
        sends, recvs = (right_send, right_recv) if to_right else (left_send, left_recv)
        side = other if c else x
        return pltpu.make_async_remote_copy(
            src_ref=mixed.at[x] if c == 0 and t == 0 else out.at[source, side],
            dst_ref=out.at[source, side],
            send_sem=sends.at[c, t],
            recv_sem=recvs.at[c, t],
            device_id=right if to_right else left,
            device_id_type=MESH,
        )

    swap = pltpu.make_async_remote_copy(
        src_ref=mixed.at[other],
        dst_ref=out.at[g, x],
        send_sem=x_send,
        recv_sem=x_recv,
        device_id=twin,
        device_id_type=MESH,
    )
    swap.start()
    mine = pltpu.make_async_copy(mixed.at[x], out.at[g, x], own_sem)
    mine.start()

    def sends_right(t):
        return (g >= t) & (g < last)

    def sends_left(t):
        return (g + t <= last) & (g > 0)

    for t in range(last):
        for c in range(2):
            if t == 0 and c:
                swap.wait_recv()
            if t:

                @pl.when(g >= t)
                def _():
                    hop(c, t - 1, True).wait_recv()

            @pl.when(sends_right(t))
            def _():
                hop(c, t, True).start()

            if t:

                @pl.when(g + t <= last)
                def _():
                    hop(c, t - 1, False).wait_recv()

            @pl.when(sends_left(t))
            def _():
                hop(c, t, False).start()

    for c in range(2):

        @pl.when(g >= last)
        def _():
            hop(c, last - 1, True).wait_recv()

        @pl.when(g <= 0)
        def _():
            hop(c, last - 1, False).wait_recv()

        for t in range(last):

            @pl.when(sends_right(t))
            def _():
                hop(c, t, True).wait_send()

            @pl.when(sends_left(t))
            def _():
                hop(c, t, False).wait_send()

    swap.wait_send()
    mine.wait()


def along_line(mixed, groups):
    dma = pltpu.SemaphoreType.DMA
    return pl.pallas_call(
        line_kernel,
        in_specs=[pl.BlockSpec(memory_space=pltpu.VMEM)],
        out_specs=pl.BlockSpec(memory_space=pl.ANY),
        out_shape=jax.ShapeDtypeStruct((groups,) + mixed.shape, mixed.dtype),
        scratch_shapes=[dma] * 3 + [dma((2, groups - 1)) for _ in range(4)],
        cost_estimate=COMM_COST,
        compiler_params=pltpu.CompilerParams(collective_id=1, has_side_effects=True),
        name="along_line",
    )(mixed)


def return_kernel(partial, gathered, out, base, own_sem, send, recv, base_send, base_recv):
    groups, feats = out.shape[1], out.shape[4]
    x, g, i = place(groups)
    steps = [(d, t) for t in range(groups) for d in range(2) if d or t]
    sides = (x, 1 - x)
    rows = [lax.rem(g + t, groups) for t in range(groups)]
    enter([(sides[d], rows[t] * INNER + i) for d, t in steps])

    def piece(d, t):
        return partial.at[:, rows[t], :, pl.ds(pl.multiple_of(sides[d] * feats, 128), feats)]

    copies = [
        pltpu.make_async_remote_copy(
            src_ref=piece(d, t),
            dst_ref=out.at[x, t],
            send_sem=send.at[d, t],
            recv_sem=recv.at[d, t],
            device_id=(sides[d], rows[t] * INNER + i),
            device_id_type=MESH,
        )
        for d, t in sorted(steps, reverse=True)
    ]
    for k in range(groups):
        copies.append(
            pltpu.make_async_remote_copy(
                src_ref=gathered.at[k, sides[1], :, g],
                dst_ref=base.at[k],
                send_sem=base_send.at[k],
                recv_sem=base_recv.at[k],
                device_id=(sides[1], g * INNER + i),
                device_id_type=MESH,
            )
        )
    for copy in copies:
        copy.start()
    mine = pltpu.make_async_copy(piece(0, 0), out.at[x, 0], own_sem)
    mine.start()
    mine.wait()
    for copy in copies:
        copy.wait_send()
    for d, t in steps:
        pltpu.make_async_remote_copy(
            src_ref=piece(d, t),
            dst_ref=out.at[sides[d], t],
            send_sem=send.at[d, t],
            recv_sem=recv.at[d, t],
            device_id=(sides[d], rows[t] * INNER + i),
            device_id_type=MESH,
        ).wait_recv()
    for copy in copies[len(steps) :]:
        copy.wait_recv()


def send_back(partial, gathered):
    groups, dp = gathered.shape[:2]
    kinds, _, half, width = gathered.shape[2:]
    feats = partial.shape[3] // dp
    dma = pltpu.SemaphoreType.DMA
    return pl.pallas_call(
        return_kernel,
        in_specs=[pl.BlockSpec(memory_space=pltpu.VMEM), pl.BlockSpec(memory_space=pl.ANY)],
        out_specs=[pl.BlockSpec(memory_space=pl.ANY)] * 2,
        out_shape=[
            jax.ShapeDtypeStruct((dp, groups, kinds, half, feats), partial.dtype),
            jax.ShapeDtypeStruct((groups, kinds, half, width), partial.dtype),
        ],
        scratch_shapes=[dma, dma((2, groups)), dma((2, groups)), dma((groups,)), dma((groups,))],
        cost_estimate=COMM_COST,
        compiler_params=pltpu.CompilerParams(collective_id=2, has_side_effects=True),
        name="send_back",
    )(partial, gathered)


def hidden_kernel(a, w, out, total):
    step = pl.program_id(1)
    left = jnp.concatenate([a[j, 0] for j in range(a.shape[0])], axis=1)
    depth, hid = left.shape[1], w.shape[4]
    product = jnp.dot(left, w[...].reshape(depth, hid), preferred_element_type=jnp.float32)

    @pl.when(step == 0)
    def _():
        total[...] = product

    @pl.when(step > 0)
    def _():
        total[...] += product

    @pl.when(step == pl.num_programs(1) - 1)
    def _():
        rows = total.shape[0] // 2
        value, tangent = gelu_pair(total[:rows], total[rows:])
        out[:rows] = value.astype(jnp.bfloat16)
        out[rows:] = tangent.astype(jnp.bfloat16)


def hidden_layer(gathered, w, dp):
    groups, _, rows, width = gathered.shape
    deep, hid = w.shape[3:]
    per = groups // dp
    return pl.pallas_call(
        hidden_kernel,
        grid=(dp, groups),
        in_specs=[
            pl.BlockSpec((dp, 1, rows, width), lambda f, k: (lax.rem(k, per), lax.div(k, per), 0, 0)),
            pl.BlockSpec((1, INNER, 1, deep, hid), lambda f, k: (f, 0, k, 0, 0)),
        ],
        out_specs=pl.BlockSpec((rows, hid), lambda f, k: (0, f)),
        out_shape=jax.ShapeDtypeStruct((rows, dp * hid), jnp.bfloat16),
        scratch_shapes=[pltpu.VMEM((rows, hid), jnp.float32)],
        cost_estimate=pl.CostEstimate(
            flops=2 * rows * groups * dp * width * dp * hid,
            bytes_accessed=2 * dp * INNER * groups * deep * hid,
            transcendentals=0,
        ),
        name="hidden_layer",
    )(gathered, w)


def in_layer(block, dp, seq):
    layers = [
        [d * seq + layer * INNER + i for d in range(dp) for i in range(INNER)]
        for layer in range(seq // INNER)
    ]
    return lax.all_gather(block, ("dp", "seq"), axis_index_groups=layers, axis=0, tiled=False)


def by_layers(query, key, value, d_query, d_key, d_value, residual, d_residual, w_in, w_out, dp, seq):
    groups = seq // INNER
    rows, feats = query.shape
    half, width = rows // dp, feats // groups
    w_out_layer = in_layer(w_out, dp, seq).reshape(dp * INNER * w_out.shape[0], w_out.shape[1])
    own, kv, win = spread(
        (query, d_query, residual, d_residual, key, value, d_key, d_value), w_in, groups
    )
    win, w_out_layer = lax.optimization_barrier((win, w_out_layer))
    w_in_layer = in_layer(win, dp, seq).reshape((dp, INNER) + win.shape)
    gathered = along_line(attend_wide(own, kv, dp), groups)
    hidden = hidden_layer(gathered.reshape(groups, dp, 2 * groups * half, width), w_in_layer, dp)
    partial = jnp.dot(hidden, w_out_layer, preferred_element_type=jnp.float32).astype(jnp.bfloat16)
    parts, base_other = send_back(partial.reshape(2, groups, half, dp * feats), gathered)
    x, g, _ = place(groups)
    base_own = lax.dynamic_index_in_dim(gathered, g, axis=3, keepdims=False)
    base_own = lax.dynamic_index_in_dim(base_own, x, axis=1, keepdims=False)
    base = jnp.stack([jnp.where(x == 0, base_own, base_other), jnp.where(x == 0, base_other, base_own)])
    base = base.transpose(0, 2, 3, 1, 4).reshape(2, 2, half, feats)
    total = base.astype(jnp.float32) + jnp.sum(parts.astype(jnp.float32), axis=1)
    out = total.astype(jnp.bfloat16).transpose(1, 0, 2, 3).reshape(2, rows, feats)
    return (out[0], out[1])


def on_device(*args, dp, seq):
    query, w_in = args[0], args[8]
    groups = seq // INNER
    tile = groups * HEAD_DIM
    if dp != 2 or seq % INNER or groups < 2 or groups % dp or query.shape[1] % tile or w_in.shape[1] % tile:
        return by_rows(*args)
    return by_layers(*args, dp=dp, seq=seq)


def solution(mesh):
    in_specs = (P("seq", "dp"),) * 9 + (P(("dp", "seq"), None),)
    out_specs = (P("seq", "dp"), P("seq", "dp"))
    body = functools.partial(on_device, dp=mesh.shape["dp"], seq=mesh.shape["seq"])
    return jax.shard_map(
        body, mesh=mesh, in_specs=in_specs, out_specs=out_specs, check_vma=False
    )
```

```python
import functools
import math

import jax
import jax.numpy as jnp
from jax import lax
from jax.experimental import pallas as pl
from jax.experimental.pallas import tpu as pltpu
from jax.sharding import PartitionSpec as P

HEAD_DIM = 128


gelu_coeff = 0.7978845608
cubic_coeff = 0.044715


def gelu_pair(pre_act, d_pre_act):
    inner_arg = gelu_coeff * (pre_act + cubic_coeff * pre_act * pre_act * pre_act)
    hyper = jnp.tanh(inner_arg)
    gelu_value = 0.5 * pre_act * (1.0 + hyper)
    gelu_slope = 0.5 * (1.0 + hyper) + 0.5 * pre_act * (1.0 - hyper * hyper) * gelu_coeff * (
        1.0 + 3.0 * cubic_coeff * pre_act * pre_act
    )
    return (gelu_value, gelu_slope * d_pre_act)


def nt(a, b):
    return lax.dot_general(a, b, (((1,), (1,)), ((), ())), preferred_element_type=jnp.float32)


def attend_math(q, dq, res, dres, keys, values, keys_pair, values_pair):
    scale = 1.0 / math.sqrt(HEAD_DIM)
    scores = nt(q, keys) * scale
    d_scores = nt(jnp.concatenate([dq, q], axis=1), keys_pair) * scale
    peak = jnp.max(scores, axis=1, keepdims=True)
    weights = jnp.exp(scores - peak)
    mixed = weights * d_scores
    total = jnp.sum(weights, axis=1, keepdims=True)
    slope = jnp.sum(mixed, axis=1, keepdims=True)
    both = jnp.dot(weights.astype(jnp.bfloat16), values_pair, preferred_element_type=jnp.float32)
    tangent = both[:, HEAD_DIM:] + jnp.dot(
        mixed.astype(jnp.bfloat16), values, preferred_element_type=jnp.float32
    )
    attended = both[:, :HEAD_DIM] / total
    d_attended = tangent / total - (slope / total) * attended
    return (
        (res.astype(jnp.float32) + attended).astype(jnp.bfloat16),
        (dres.astype(jnp.float32) + d_attended).astype(jnp.bfloat16),
    )


def attend_kernel(q, dq, res, dres, k, v, dk, dv, out, *, rows):
    keys, values = k[...], v[...]
    keys_pair = jnp.concatenate([keys, dk[...]], axis=1)
    values_pair = jnp.concatenate([values, dv[...]], axis=1)
    for start in range(0, q.shape[0], rows):
        part = pl.ds(start, rows)
        out[0, part, :], out[1, part, :] = attend_math(
            q[part, :], dq[part, :], res[part, :], dres[part, :],
            keys, values, keys_pair, values_pair,
        )


def attend(query, d_query, residual, d_residual, kv):
    rows, feats = query.shape
    heads = feats // HEAD_DIM
    length = kv.shape[0]
    own = pl.BlockSpec((rows, HEAD_DIM), lambda h: (0, h))

    def kv_spec(i):
        return pl.BlockSpec((length, HEAD_DIM), lambda h: (0, i * heads + h))

    return pl.pallas_call(
        functools.partial(attend_kernel, rows=min(rows, 128)),
        grid=(heads,),
        in_specs=[own] * 4 + [kv_spec(i) for i in range(4)],
        out_specs=pl.BlockSpec((2, rows, HEAD_DIM), lambda h: (0, 0, h)),
        out_shape=jax.ShapeDtypeStruct((2, rows, feats), jnp.bfloat16),
        cost_estimate=pl.CostEstimate(
            flops=12 * rows * length * feats, bytes_accessed=8 * length * feats, transcendentals=0
        ),
        name="attend",
    )(query, d_query, residual, d_residual, kv, kv, kv, kv)


def by_rows(query, key, value, d_query, d_key, d_value, residual, d_residual, w_in, w_out):
    rows, feats = query.shape
    kv = lax.all_gather(
        jnp.concatenate([key, value, d_key, d_value], axis=1), "seq", axis=0, tiled=True
    )
    w_in_whole = lax.all_gather(w_in, "seq", axis=0, tiled=True)
    w_out_whole = lax.all_gather(w_out, "seq", axis=0, tiled=True)
    mixed = attend(query, d_query, residual, d_residual, kv).reshape(2 * rows, feats)
    whole = lax.all_gather(mixed, "dp", axis=1, tiled=True)
    pre = jnp.dot(whole, w_in_whole, preferred_element_type=jnp.float32)
    hidden, d_hidden = gelu_pair(pre[:rows], pre[rows:])
    hidden = jnp.concatenate([hidden.astype(jnp.bfloat16), d_hidden.astype(jnp.bfloat16)], axis=0)
    partial = jnp.dot(hidden, w_out_whole, preferred_element_type=jnp.float32)
    summed = lax.psum_scatter(
        partial.astype(jnp.bfloat16), "dp", scatter_dimension=1, tiled=True
    ).astype(jnp.float32)
    out = (mixed.astype(jnp.float32) + summed).astype(jnp.bfloat16)
    return (out[:rows], out[rows:])


INNER = 4
MESH = pl.DeviceIdType.MESH
COMM_COST = pl.CostEstimate(flops=10**11, bytes_accessed=10**8, transcendentals=0)


def place(groups):
    seq = lax.axis_index("seq")
    return lax.axis_index("dp"), lax.div(seq, INNER), lax.rem(seq, INNER)


def enter(devices):
    barrier = pltpu.get_barrier_semaphore()
    for device in devices:
        pl.semaphore_signal(barrier, inc=1, device_id=device, device_id_type=MESH)
    pl.semaphore_wait(barrier, len(devices))


def spread_kernel(
    q, dq, res, dres, k, v, dk, dv, own, kv, z_send, z_recv, own_sem,
    p_send, p_recv, y_send, y_recv, f_send, f_recv,
):
    groups, width = own.shape[1], own.shape[3]
    x, g, i = place(groups)
    partner = (x, g * INNER + i + 1 - 2 * lax.rem(i, 2))
    across_i = lax.rem(i + 2, INNER)
    across = (x, g * INNER + across_i)
    peers = [(x, lax.rem(g + t, groups) * INNER + i) for t in range(1, groups)]
    enter(peers + [partner, across])

    def piece(j, to):
        if j < 4:
            return (k, v, dk, dv)[j].at[:, pl.ds(pl.multiple_of(to * width, 128), width)]
        return (q, dq, res, dres)[j - 4].at[:, pl.ds(pl.multiple_of(to * width, 128), width)]

    def slot(j, source):
        if j < 4:
            return kv.at[i, source, j]
        return own.at[j - 4, source]

    def over_z(t, j):
        return pltpu.make_async_remote_copy(
            src_ref=piece(j, lax.rem(g + t, groups)),
            dst_ref=slot(j, g),
            send_sem=z_send.at[t - 1, j],
            recv_sem=z_recv.at[t - 1, j],
            device_id=peers[t - 1],
            device_id_type=MESH,
        )

    def layer(block, source, send, recv, t, device):
        return pltpu.make_async_remote_copy(
            src_ref=kv.at[block, source],
            dst_ref=kv.at[block, source],
            send_sem=send.at[t],
            recv_sem=recv.at[t],
            device_id=device,
            device_id_type=MESH,
        )

    z_copies = {}
    for t in range(1, groups):
        for j in range(8):
            z_copies[t, j] = over_z(t, j)
            z_copies[t, j].start()
    locals_ = [pltpu.make_async_copy(piece(j, g), slot(j, g), own_sem.at[j]) for j in range(8)]
    for copy in locals_:
        copy.start()
    for copy in locals_:
        copy.wait()
    inside, forwards = [], []

    def forward(t):
        inside[t][1].wait_recv()
        source = lax.rem(g + groups - t, groups)
        copy = layer(across_i, source, f_send, f_recv, t, partner)
        copy.start()
        forwards.append(copy)

    for t in range(groups):
        if t:
            for j in range(4):
                z_copies[t, j].wait_recv()
        source = lax.rem(g + groups - t, groups)
        pair = (
            layer(i, source, p_send, p_recv, t, partner),
            layer(i, source, y_send, y_recv, t, across),
        )
        pair[1].start()
        pair[0].start()
        inside.append(pair)
        if t:
            forward(t - 1)
    forward(groups - 1)
    for t in range(groups):
        inside[t][0].wait()
        inside[t][1].wait_send()
        forwards[t].wait()
    for (t, j), copy in z_copies.items():
        copy.wait_send()
        if j >= 4:
            copy.wait_recv()


def spread(tensors, groups):
    rows, feats = tensors[0].shape
    width = feats // groups
    dma = pltpu.SemaphoreType.DMA
    return pl.pallas_call(
        spread_kernel,
        in_specs=[pl.BlockSpec(memory_space=pltpu.VMEM)] * 8,
        out_specs=[pl.BlockSpec(memory_space=pl.ANY)] * 2,
        out_shape=[
            jax.ShapeDtypeStruct((4, groups, rows, width), jnp.bfloat16),
            jax.ShapeDtypeStruct((INNER, groups, 4, rows, width), jnp.bfloat16),
        ],
        scratch_shapes=[dma((groups - 1, 8)), dma((groups - 1, 8)), dma((8,))]
        + [dma((groups,)) for _ in range(6)],
        cost_estimate=COMM_COST,
        compiler_params=pltpu.CompilerParams(collective_id=0, has_side_effects=True),
        name="spread",
    )(*tensors)


def columns_kernel(w_in, win, own_sem, send, recv):
    groups, _, hid = win.shape
    x, g, i = place(groups)
    rows = [lax.rem(g + t, groups) for t in range(groups)]
    enter([(x, rows[t] * INNER + i) for t in range(1, groups)])

    def piece(t):
        return w_in.at[:, pl.ds(pl.multiple_of(rows[t] * hid, 128), hid)]

    copies = [
        pltpu.make_async_remote_copy(
            src_ref=piece(t),
            dst_ref=win.at[g],
            send_sem=send.at[t - 1],
            recv_sem=recv.at[t - 1],
            device_id=(x, rows[t] * INNER + i),
            device_id_type=MESH,
        )
        for t in range(1, groups)
    ]
    for copy in copies:
        copy.start()
    mine = pltpu.make_async_copy(piece(0), win.at[g], own_sem)
    mine.start()
    mine.wait()
    for copy in copies:
        copy.wait()


def columns(w_in, groups):
    dma = pltpu.SemaphoreType.DMA
    return pl.pallas_call(
        columns_kernel,
        in_specs=[pl.BlockSpec(memory_space=pltpu.VMEM)],
        out_specs=pl.BlockSpec(memory_space=pl.ANY),
        out_shape=jax.ShapeDtypeStruct(
            (groups, w_in.shape[0], w_in.shape[1] // groups), jnp.bfloat16
        ),
        scratch_shapes=[dma, dma((groups - 1,)), dma((groups - 1,))],
        cost_estimate=COMM_COST,
        compiler_params=pltpu.CompilerParams(collective_id=3, has_side_effects=True),
        name="columns",
    )(w_in)


def attend_wide_kernel(q, dq, res, dres, k, v, dk, dv, out):
    length = k.shape[0] * k.shape[1] * k.shape[3]
    keys, values, d_keys, d_values = (
        ref[...].reshape(length, HEAD_DIM) for ref in (k, v, dk, dv)
    )
    keys_pair = jnp.concatenate([keys, d_keys], axis=1)
    values_pair = jnp.concatenate([values, d_values], axis=1)
    half = out.shape[3]
    for g in range(q.shape[1]):
        pair = attend_math(
            q[0, g], dq[0, g], res[0, g], dres[0, g], keys, values, keys_pair, values_pair
        )
        for side in range(out.shape[0]):
            for kind in range(2):
                out[side, kind, g] = pair[kind][side * half : (side + 1) * half]


def attend_wide(own, kv, sides):
    _, groups, rows, width = own.shape
    heads = width // HEAD_DIM
    half = rows // sides

    def own_spec(i):
        return pl.BlockSpec((1, groups, rows, HEAD_DIM), lambda h: (i, 0, 0, h))

    def kv_spec(i):
        return pl.BlockSpec((INNER, groups, 1, rows, HEAD_DIM), lambda h: (0, 0, i, 0, h))

    return pl.pallas_call(
        attend_wide_kernel,
        grid=(heads,),
        in_specs=[own_spec(i) for i in range(4)] + [kv_spec(i) for i in range(4)],
        out_specs=pl.BlockSpec((sides, 2, groups, half, HEAD_DIM), lambda h: (0, 0, 0, 0, h)),
        out_shape=jax.ShapeDtypeStruct((sides, 2, groups, half, width), jnp.bfloat16),
        cost_estimate=pl.CostEstimate(
            flops=12 * INNER * (groups * rows) ** 2 * width,
            bytes_accessed=8 * INNER * groups * rows * width,
            transcendentals=0,
        ),
        name="attend_wide",
    )(own, own, own, own, kv, kv, kv, kv)


def line_kernel(
    mixed, out, own_sem, x_send, x_recv, right_send, right_recv, left_send, left_recv
):
    groups = out.shape[0]
    x, g, i = place(groups)
    last = groups - 1
    other = 1 - x
    right = (x, jnp.minimum(g + 1, last) * INNER + i)
    left = (x, jnp.maximum(g - 1, 0) * INNER + i)
    twin = (other, g * INNER + i)
    enter([(x, lax.rem(g + t, groups) * INNER + i) for t in range(1, groups)] + [twin])

    def hop(c, t, to_right):
        source = g - t if to_right else g + t
        sends, recvs = (right_send, right_recv) if to_right else (left_send, left_recv)
        side = other if c else x
        return pltpu.make_async_remote_copy(
            src_ref=mixed.at[x] if c == 0 and t == 0 else out.at[source, side],
            dst_ref=out.at[source, side],
            send_sem=sends.at[c, t],
            recv_sem=recvs.at[c, t],
            device_id=right if to_right else left,
            device_id_type=MESH,
        )

    swap = pltpu.make_async_remote_copy(
        src_ref=mixed.at[other],
        dst_ref=out.at[g, x],
        send_sem=x_send,
        recv_sem=x_recv,
        device_id=twin,
        device_id_type=MESH,
    )
    swap.start()
    mine = pltpu.make_async_copy(mixed.at[x], out.at[g, x], own_sem)
    mine.start()

    def sends_right(t):
        return (g >= t) & (g < last)

    def sends_left(t):
        return (g + t <= last) & (g > 0)

    for t in range(last):
        for c in range(2):
            if t == 0 and c:
                swap.wait_recv()
            if t:

                @pl.when(g >= t)
                def _():
                    hop(c, t - 1, True).wait_recv()

            @pl.when(sends_right(t))
            def _():
                hop(c, t, True).start()

            if t:

                @pl.when(g + t <= last)
                def _():
                    hop(c, t - 1, False).wait_recv()

            @pl.when(sends_left(t))
            def _():
                hop(c, t, False).start()

    for c in range(2):

        @pl.when(g >= last)
        def _():
            hop(c, last - 1, True).wait_recv()

        @pl.when(g <= 0)
        def _():
            hop(c, last - 1, False).wait_recv()

        for t in range(last):

            @pl.when(sends_right(t))
            def _():
                hop(c, t, True).wait_send()

            @pl.when(sends_left(t))
            def _():
                hop(c, t, False).wait_send()

    swap.wait_send()
    mine.wait()


def along_line(mixed, groups):
    dma = pltpu.SemaphoreType.DMA
    return pl.pallas_call(
        line_kernel,
        in_specs=[pl.BlockSpec(memory_space=pltpu.VMEM)],
        out_specs=pl.BlockSpec(memory_space=pl.ANY),
        out_shape=jax.ShapeDtypeStruct((groups,) + mixed.shape, mixed.dtype),
        scratch_shapes=[dma] * 3 + [dma((2, groups - 1)) for _ in range(4)],
        cost_estimate=COMM_COST,
        compiler_params=pltpu.CompilerParams(collective_id=1, has_side_effects=True),
        name="along_line",
    )(mixed)


def return_kernel(
    partial, gathered, out, base, theirs, joined, own_sem, p_send, p_recv, send, recv,
    base_send, base_recv,
):
    groups, feats = base.shape[0], out.shape[4]
    kinds = out.shape[2]
    x, g, i = place(groups)
    sides = (x, 1 - x)
    near = g + 1 - 2 * lax.rem(g, 2)
    far = lax.rem(g + 2, groups)
    near_far = lax.rem(near + 2, groups)
    ends = (g, near, far)
    steps = [(d, e) for e in range(3) for d in range(2) if d or e]
    enter([(sides[d], ends[e] * INNER + i) for d, e in steps])

    def part(d):
        return pl.ds(pl.multiple_of(sides[d] * feats, 128), feats)

    def remote(src, dst, send_sem, recv_sem, d, row):
        return pltpu.make_async_remote_copy(
            src_ref=src,
            dst_ref=dst,
            send_sem=send_sem,
            recv_sem=recv_sem,
            device_id=(sides[d], row * INNER + i),
            device_id_type=MESH,
        )

    def final(d, e, kind):
        source = joined.at[kind] if e == 2 else partial.at[kind, ends[e]]
        return remote(
            source.at[:, part(d)],
            out.at[x, e, kind],
            send.at[d, e, kind],
            recv.at[d, e, kind],
            d,
            ends[e],
        )

    def arrival(d, e, kind):
        return remote(
            partial.at[kind, ends[0], :, part(d)],
            out.at[sides[d], e, kind],
            send.at[d, e, kind],
            recv.at[d, e, kind],
            d,
            ends[e],
        )

    across = [
        remote(
            partial.at[kind, near_far], theirs.at[kind], p_send.at[kind], p_recv.at[kind], 0, near
        )
        for kind in range(kinds)
    ]
    bases = [
        remote(
            gathered.at[k, sides[1], :, g], base.at[k], base_send.at[k], base_recv.at[k], 1, g
        )
        for k in range(groups)
    ]
    sent = [final(1, 0, kind) for kind in range(kinds)]
    for copy in across + sent + bases:
        copy.start()
    mine = [
        pltpu.make_async_copy(
            partial.at[kind, g, :, part(0)], out.at[x, 0, kind], own_sem.at[kind]
        )
        for kind in range(kinds)
    ]
    for copy in mine:
        copy.start()
    for kind in range(kinds):
        across[kind].wait_recv()
        joined[kind] = (
            partial[kind, far].astype(jnp.float32) + theirs[kind].astype(jnp.float32)
        ).astype(jnp.bfloat16)
        for e in (2, 1):
            for d in range(2):
                copy = final(d, e, kind)
                copy.start()
                sent.append(copy)
    for copy in mine:
        copy.wait()
    for copy in across + sent:
        copy.wait_send()
    for kind in range(kinds):
        for d, e in steps:
            arrival(d, e, kind).wait_recv()
    for copy in bases:
        copy.wait()


def send_back(partial, gathered):
    groups, dp = gathered.shape[:2]
    kinds, _, half, width = gathered.shape[2:]
    feats = partial.shape[3] // dp
    dma = pltpu.SemaphoreType.DMA
    return pl.pallas_call(
        return_kernel,
        in_specs=[pl.BlockSpec(memory_space=pltpu.VMEM), pl.BlockSpec(memory_space=pl.ANY)],
        out_specs=[pl.BlockSpec(memory_space=pl.ANY)] * 2,
        out_shape=[
            jax.ShapeDtypeStruct((dp, 3, kinds, half, feats), partial.dtype),
            jax.ShapeDtypeStruct((groups, kinds, half, width), partial.dtype),
        ],
        scratch_shapes=[pltpu.VMEM((kinds, half, dp * feats), jnp.bfloat16) for _ in range(2)]
        + [dma((kinds,)) for _ in range(3)]
        + [dma((2, 3, kinds)), dma((2, 3, kinds)), dma((groups,)), dma((groups,))],
        cost_estimate=COMM_COST,
        compiler_params=pltpu.CompilerParams(collective_id=2, has_side_effects=True),
        name="send_back",
    )(partial, gathered)


def hidden_kernel(a, w, out, total):
    step = pl.program_id(1)
    left = jnp.concatenate([a[j, 0] for j in range(a.shape[0])], axis=1)
    depth, hid = left.shape[1], w.shape[4]
    product = jnp.dot(left, w[...].reshape(depth, hid), preferred_element_type=jnp.float32)

    @pl.when(step == 0)
    def _():
        total[...] = product

    @pl.when(step > 0)
    def _():
        total[...] += product

    @pl.when(step == pl.num_programs(1) - 1)
    def _():
        rows = total.shape[0] // 2
        value, tangent = gelu_pair(total[:rows], total[rows:])
        out[:rows] = value.astype(jnp.bfloat16)
        out[rows:] = tangent.astype(jnp.bfloat16)


def hidden_layer(gathered, w, dp):
    groups, _, rows, width = gathered.shape
    deep, hid = w.shape[3:]
    per = groups // dp
    return pl.pallas_call(
        hidden_kernel,
        grid=(dp, groups),
        in_specs=[
            pl.BlockSpec((dp, 1, rows, width), lambda f, k: (lax.rem(k, per), lax.div(k, per), 0, 0)),
            pl.BlockSpec((1, INNER, 1, deep, hid), lambda f, k: (f, 0, k, 0, 0)),
        ],
        out_specs=pl.BlockSpec((rows, hid), lambda f, k: (0, f)),
        out_shape=jax.ShapeDtypeStruct((rows, dp * hid), jnp.bfloat16),
        scratch_shapes=[pltpu.VMEM((rows, hid), jnp.float32)],
        cost_estimate=pl.CostEstimate(
            flops=2 * rows * groups * dp * width * dp * hid,
            bytes_accessed=2 * dp * INNER * groups * deep * hid,
            transcendentals=0,
        ),
        name="hidden_layer",
    )(gathered, w)


def in_layer(block, dp, seq):
    layers = [
        [d * seq + layer * INNER + i for d in range(dp) for i in range(INNER)]
        for layer in range(seq // INNER)
    ]
    return lax.all_gather(block, ("dp", "seq"), axis_index_groups=layers, axis=0, tiled=False)


def by_layers(query, key, value, d_query, d_key, d_value, residual, d_residual, w_in, w_out, dp, seq):
    groups = seq // INNER
    rows, feats = query.shape
    half, width = rows // dp, feats // groups
    w_out_layer = in_layer(w_out, dp, seq).reshape(dp * INNER * w_out.shape[0], w_out.shape[1])
    tensors = (query, d_query, residual, d_residual, key, value, d_key, d_value)
    win, tensors = lax.optimization_barrier((columns(w_in, groups), tensors))
    own, kv = spread(tensors, groups)
    w_in_layer = in_layer(win, dp, seq).reshape((dp, INNER) + win.shape)
    gathered = along_line(attend_wide(own, kv, dp), groups)
    hidden = hidden_layer(gathered.reshape(groups, dp, 2 * groups * half, width), w_in_layer, dp)
    partial = jnp.dot(hidden, w_out_layer, preferred_element_type=jnp.float32).astype(jnp.bfloat16)
    parts, base_other = send_back(partial.reshape(2, groups, half, dp * feats), gathered)
    x, g, _ = place(groups)
    base_own = lax.dynamic_index_in_dim(gathered, g, axis=3, keepdims=False)
    base_own = lax.dynamic_index_in_dim(base_own, x, axis=1, keepdims=False)
    base = jnp.stack([jnp.where(x == 0, base_own, base_other), jnp.where(x == 0, base_other, base_own)])
    base = base.transpose(0, 2, 3, 1, 4).reshape(2, 2, half, feats)
    total = base.astype(jnp.float32) + jnp.sum(parts.astype(jnp.float32), axis=1)
    out = total.astype(jnp.bfloat16).transpose(1, 0, 2, 3).reshape(2, rows, feats)
    return (out[0], out[1])


def on_device(*args, dp, seq):
    query, w_in = args[0], args[8]
    groups = seq // INNER
    tile = groups * HEAD_DIM
    if dp != 2 or seq % INNER or groups != 4 or query.shape[1] % tile or w_in.shape[1] % tile:
        return by_rows(*args)
    return by_layers(*args, dp=dp, seq=seq)


def solution(mesh):
    in_specs = (P("seq", "dp"),) * 9 + (P(("dp", "seq"), None),)
    out_specs = (P("seq", "dp"), P("seq", "dp"))
    body = functools.partial(on_device, dp=mesh.shape["dp"], seq=mesh.shape["seq"])
    return jax.shard_map(
        body, mesh=mesh, in_specs=in_specs, out_specs=out_specs, check_vma=False
    )
```

```python
import functools
import math

import jax
import jax.numpy as jnp
from jax import lax
from jax.experimental import pallas as pl
from jax.experimental.pallas import tpu as pltpu
from jax.sharding import PartitionSpec as P

HEAD_DIM = 128


gelu_coeff = 0.7978845608
cubic_coeff = 0.044715


def gelu_pair(pre_act, d_pre_act):
    inner_arg = gelu_coeff * (pre_act + cubic_coeff * pre_act * pre_act * pre_act)
    hyper = jnp.tanh(inner_arg)
    gelu_value = 0.5 * pre_act * (1.0 + hyper)
    gelu_slope = 0.5 * (1.0 + hyper) + 0.5 * pre_act * (1.0 - hyper * hyper) * gelu_coeff * (
        1.0 + 3.0 * cubic_coeff * pre_act * pre_act
    )
    return (gelu_value, gelu_slope * d_pre_act)


def nt(a, b):
    return lax.dot_general(a, b, (((1,), (1,)), ((), ())), preferred_element_type=jnp.float32)


def attend_math(q, dq, res, dres, keys, values, keys_pair, values_pair):
    scale = 1.0 / math.sqrt(HEAD_DIM)
    scores = nt(q, keys) * scale
    d_scores = nt(jnp.concatenate([dq, q], axis=1), keys_pair) * scale
    peak = jnp.max(scores, axis=1, keepdims=True)
    weights = jnp.exp(scores - peak)
    mixed = weights * d_scores
    total = jnp.sum(weights, axis=1, keepdims=True)
    slope = jnp.sum(mixed, axis=1, keepdims=True)
    both = jnp.dot(weights.astype(jnp.bfloat16), values_pair, preferred_element_type=jnp.float32)
    tangent = both[:, HEAD_DIM:] + jnp.dot(
        mixed.astype(jnp.bfloat16), values, preferred_element_type=jnp.float32
    )
    attended = both[:, :HEAD_DIM] / total
    d_attended = tangent / total - (slope / total) * attended
    return (
        (res.astype(jnp.float32) + attended).astype(jnp.bfloat16),
        (dres.astype(jnp.float32) + d_attended).astype(jnp.bfloat16),
    )


def attend_kernel(q, dq, res, dres, k, v, dk, dv, out, *, rows):
    keys, values = k[...], v[...]
    keys_pair = jnp.concatenate([keys, dk[...]], axis=1)
    values_pair = jnp.concatenate([values, dv[...]], axis=1)
    for start in range(0, q.shape[0], rows):
        part = pl.ds(start, rows)
        out[0, part, :], out[1, part, :] = attend_math(
            q[part, :], dq[part, :], res[part, :], dres[part, :],
            keys, values, keys_pair, values_pair,
        )


def attend(query, d_query, residual, d_residual, kv):
    rows, feats = query.shape
    heads = feats // HEAD_DIM
    length = kv.shape[0]
    own = pl.BlockSpec((rows, HEAD_DIM), lambda h: (0, h))

    def kv_spec(i):
        return pl.BlockSpec((length, HEAD_DIM), lambda h: (0, i * heads + h))

    return pl.pallas_call(
        functools.partial(attend_kernel, rows=min(rows, 128)),
        grid=(heads,),
        in_specs=[own] * 4 + [kv_spec(i) for i in range(4)],
        out_specs=pl.BlockSpec((2, rows, HEAD_DIM), lambda h: (0, 0, h)),
        out_shape=jax.ShapeDtypeStruct((2, rows, feats), jnp.bfloat16),
        cost_estimate=pl.CostEstimate(
            flops=12 * rows * length * feats, bytes_accessed=8 * length * feats, transcendentals=0
        ),
        name="attend",
    )(query, d_query, residual, d_residual, kv, kv, kv, kv)


def by_rows(query, key, value, d_query, d_key, d_value, residual, d_residual, w_in, w_out):
    rows, feats = query.shape
    kv = lax.all_gather(
        jnp.concatenate([key, value, d_key, d_value], axis=1), "seq", axis=0, tiled=True
    )
    w_in_whole = lax.all_gather(w_in, "seq", axis=0, tiled=True)
    w_out_whole = lax.all_gather(w_out, "seq", axis=0, tiled=True)
    mixed = attend(query, d_query, residual, d_residual, kv).reshape(2 * rows, feats)
    whole = lax.all_gather(mixed, "dp", axis=1, tiled=True)
    pre = jnp.dot(whole, w_in_whole, preferred_element_type=jnp.float32)
    hidden, d_hidden = gelu_pair(pre[:rows], pre[rows:])
    hidden = jnp.concatenate([hidden.astype(jnp.bfloat16), d_hidden.astype(jnp.bfloat16)], axis=0)
    partial = jnp.dot(hidden, w_out_whole, preferred_element_type=jnp.float32)
    summed = lax.psum_scatter(
        partial.astype(jnp.bfloat16), "dp", scatter_dimension=1, tiled=True
    ).astype(jnp.float32)
    out = (mixed.astype(jnp.float32) + summed).astype(jnp.bfloat16)
    return (out[:rows], out[rows:])


INNER = 4
MESH = pl.DeviceIdType.MESH
COMM_COST = pl.CostEstimate(flops=10**11, bytes_accessed=10**8, transcendentals=0)


def place(groups):
    seq = lax.axis_index("seq")
    return lax.axis_index("dp"), lax.div(seq, INNER), lax.rem(seq, INNER)


def enter(devices):
    barrier = pltpu.get_barrier_semaphore()
    for device in devices:
        pl.semaphore_signal(barrier, inc=1, device_id=device, device_id_type=MESH)
    pl.semaphore_wait(barrier, len(devices))


def spread_kernel(
    q, dq, res, dres, k, v, dk, dv, w_in, own, kv, win, z_send, z_recv, own_sem,
    p_send, p_recv, y_send, y_recv, f_send, f_recv,
):
    groups, width = own.shape[1], own.shape[3]
    hid = win.shape[2]
    x, g, i = place(groups)
    partner = (x, g * INNER + i + 1 - 2 * lax.rem(i, 2))
    across_i = lax.rem(i + 2, INNER)
    across = (x, g * INNER + across_i)
    peers = [(x, lax.rem(g + t, groups) * INNER + i) for t in range(1, groups)]
    enter(peers + [partner, across])

    def piece(j, to):
        if j < 4:
            return (k, v, dk, dv)[j].at[:, pl.ds(pl.multiple_of(to * width, 128), width)]
        if j < 8:
            return (q, dq, res, dres)[j - 4].at[:, pl.ds(pl.multiple_of(to * width, 128), width)]
        return w_in.at[:, pl.ds(pl.multiple_of(to * hid, 128), hid)]

    def slot(j, source):
        if j < 4:
            return kv.at[i, source, j]
        if j < 8:
            return own.at[j - 4, source]
        return win.at[source]

    def over_z(t, j):
        return pltpu.make_async_remote_copy(
            src_ref=piece(j, lax.rem(g + t, groups)),
            dst_ref=slot(j, g),
            send_sem=z_send.at[t - 1, j],
            recv_sem=z_recv.at[t - 1, j],
            device_id=peers[t - 1],
            device_id_type=MESH,
        )

    def layer(block, source, send, recv, t, device):
        return pltpu.make_async_remote_copy(
            src_ref=kv.at[block, source],
            dst_ref=kv.at[block, source],
            send_sem=send.at[t],
            recv_sem=recv.at[t],
            device_id=device,
            device_id_type=MESH,
        )

    z_copies = {}
    for order in (range(8), (8,)):
        for t in range(1, groups):
            for j in order:
                z_copies[t, j] = over_z(t, j)
                z_copies[t, j].start()
    locals_ = [pltpu.make_async_copy(piece(j, g), slot(j, g), own_sem.at[j]) for j in range(9)]
    for copy in locals_:
        copy.start()
    for copy in locals_:
        copy.wait()
    inside, forwards = [], []

    def forward(t):
        inside[t][1].wait_recv()
        source = lax.rem(g + groups - t, groups)
        copy = layer(across_i, source, f_send, f_recv, t, partner)
        copy.start()
        forwards.append(copy)

    for t in range(groups):
        if t:
            for j in range(4):
                z_copies[t, j].wait_recv()
        source = lax.rem(g + groups - t, groups)
        pair = (
            layer(i, source, p_send, p_recv, t, partner),
            layer(i, source, y_send, y_recv, t, across),
        )
        pair[1].start()
        pair[0].start()
        inside.append(pair)
        if t:
            forward(t - 1)
    forward(groups - 1)
    for t in range(groups):
        inside[t][0].wait()
        inside[t][1].wait_send()
        forwards[t].wait()
    for (t, j), copy in z_copies.items():
        copy.wait_send()
        if j >= 4:
            copy.wait_recv()


def spread(tensors, w_in, groups):
    rows, feats = tensors[0].shape
    width = feats // groups
    deep, hid = w_in.shape[0], w_in.shape[1] // groups
    dma = pltpu.SemaphoreType.DMA
    return pl.pallas_call(
        spread_kernel,
        in_specs=[pl.BlockSpec(memory_space=pltpu.VMEM)] * 9,
        out_specs=[pl.BlockSpec(memory_space=pl.ANY)] * 3,
        out_shape=[
            jax.ShapeDtypeStruct((4, groups, rows, width), jnp.bfloat16),
            jax.ShapeDtypeStruct((INNER, groups, 4, rows, width), jnp.bfloat16),
            jax.ShapeDtypeStruct((groups, deep, hid), jnp.bfloat16),
        ],
        scratch_shapes=[dma((groups - 1, 9)), dma((groups - 1, 9)), dma((9,))]
        + [dma((groups,)) for _ in range(6)],
        cost_estimate=COMM_COST,
        compiler_params=pltpu.CompilerParams(collective_id=0, has_side_effects=True),
        name="spread",
    )(*tensors, w_in)


def attend_wide_kernel(q, dq, res, dres, k, v, dk, dv, out):
    length = k.shape[0] * k.shape[1] * k.shape[3]
    keys, values, d_keys, d_values = (
        ref[...].reshape(length, HEAD_DIM) for ref in (k, v, dk, dv)
    )
    keys_pair = jnp.concatenate([keys, d_keys], axis=1)
    values_pair = jnp.concatenate([values, d_values], axis=1)
    half = out.shape[3]
    for g in range(q.shape[1]):
        pair = attend_math(
            q[0, g], dq[0, g], res[0, g], dres[0, g], keys, values, keys_pair, values_pair
        )
        for side in range(out.shape[0]):
            for kind in range(2):
                out[side, kind, g] = pair[kind][side * half : (side + 1) * half]


def attend_wide(own, kv, sides):
    _, groups, rows, width = own.shape
    heads = width // HEAD_DIM
    half = rows // sides

    def own_spec(i):
        return pl.BlockSpec((1, groups, rows, HEAD_DIM), lambda h: (i, 0, 0, h))

    def kv_spec(i):
        return pl.BlockSpec((INNER, groups, 1, rows, HEAD_DIM), lambda h: (0, 0, i, 0, h))

    return pl.pallas_call(
        attend_wide_kernel,
        grid=(heads,),
        in_specs=[own_spec(i) for i in range(4)] + [kv_spec(i) for i in range(4)],
        out_specs=pl.BlockSpec((sides, 2, groups, half, HEAD_DIM), lambda h: (0, 0, 0, 0, h)),
        out_shape=jax.ShapeDtypeStruct((sides, 2, groups, half, width), jnp.bfloat16),
        cost_estimate=pl.CostEstimate(
            flops=12 * INNER * (groups * rows) ** 2 * width,
            bytes_accessed=8 * INNER * groups * rows * width,
            transcendentals=0,
        ),
        name="attend_wide",
    )(own, own, own, own, kv, kv, kv, kv)


def line_kernel(
    mixed, out, own_sem, x_send, x_recv, right_send, right_recv, left_send, left_recv
):
    groups = out.shape[0]
    x, g, i = place(groups)
    last = groups - 1
    other = 1 - x
    right = (x, jnp.minimum(g + 1, last) * INNER + i)
    left = (x, jnp.maximum(g - 1, 0) * INNER + i)
    twin = (other, g * INNER + i)
    enter([(x, lax.rem(g + t, groups) * INNER + i) for t in range(1, groups)] + [twin])

    def hop(c, t, to_right):
        source = g - t if to_right else g + t
        sends, recvs = (right_send, right_recv) if to_right else (left_send, left_recv)
        side = other if c else x
        return pltpu.make_async_remote_copy(
            src_ref=mixed.at[x] if c == 0 and t == 0 else out.at[source, side],
            dst_ref=out.at[source, side],
            send_sem=sends.at[c, t],
            recv_sem=recvs.at[c, t],
            device_id=right if to_right else left,
            device_id_type=MESH,
        )

    swap = pltpu.make_async_remote_copy(
        src_ref=mixed.at[other],
        dst_ref=out.at[g, x],
        send_sem=x_send,
        recv_sem=x_recv,
        device_id=twin,
        device_id_type=MESH,
    )
    swap.start()
    mine = pltpu.make_async_copy(mixed.at[x], out.at[g, x], own_sem)
    mine.start()

    def sends_right(t):
        return (g >= t) & (g < last)

    def sends_left(t):
        return (g + t <= last) & (g > 0)

    for t in range(last):
        for c in range(2):
            if t == 0 and c:
                swap.wait_recv()
            if t:

                @pl.when(g >= t)
                def _():
                    hop(c, t - 1, True).wait_recv()

            @pl.when(sends_right(t))
            def _():
                hop(c, t, True).start()

            if t:

                @pl.when(g + t <= last)
                def _():
                    hop(c, t - 1, False).wait_recv()

            @pl.when(sends_left(t))
            def _():
                hop(c, t, False).start()

    for c in range(2):

        @pl.when(g >= last)
        def _():
            hop(c, last - 1, True).wait_recv()

        @pl.when(g <= 0)
        def _():
            hop(c, last - 1, False).wait_recv()

        for t in range(last):

            @pl.when(sends_right(t))
            def _():
                hop(c, t, True).wait_send()

            @pl.when(sends_left(t))
            def _():
                hop(c, t, False).wait_send()

    swap.wait_send()
    mine.wait()


def along_line(mixed, groups):
    dma = pltpu.SemaphoreType.DMA
    return pl.pallas_call(
        line_kernel,
        in_specs=[pl.BlockSpec(memory_space=pltpu.VMEM)],
        out_specs=pl.BlockSpec(memory_space=pl.ANY),
        out_shape=jax.ShapeDtypeStruct((groups,) + mixed.shape, mixed.dtype),
        scratch_shapes=[dma] * 3 + [dma((2, groups - 1)) for _ in range(4)],
        cost_estimate=COMM_COST,
        compiler_params=pltpu.CompilerParams(collective_id=1, has_side_effects=True),
        name="along_line",
    )(mixed)


def return_kernel(
    partial, gathered, out, base, theirs, joined, own_sem, p_send, p_recv, send, recv,
    base_send, base_recv,
):
    groups, feats = base.shape[0], out.shape[4]
    kinds = out.shape[2]
    x, g, i = place(groups)
    sides = (x, 1 - x)
    near = g + 1 - 2 * lax.rem(g, 2)
    far = lax.rem(g + 2, groups)
    near_far = lax.rem(near + 2, groups)
    ends = (g, near, far)
    steps = [(d, e) for e in range(3) for d in range(2) if d or e]
    enter([(sides[d], ends[e] * INNER + i) for d, e in steps])

    def part(d):
        return pl.ds(pl.multiple_of(sides[d] * feats, 128), feats)

    def remote(src, dst, send_sem, recv_sem, d, row):
        return pltpu.make_async_remote_copy(
            src_ref=src,
            dst_ref=dst,
            send_sem=send_sem,
            recv_sem=recv_sem,
            device_id=(sides[d], row * INNER + i),
            device_id_type=MESH,
        )

    def final(d, e, kind):
        source = joined.at[kind] if e == 2 else partial.at[kind, ends[e]]
        return remote(
            source.at[:, part(d)],
            out.at[x, e, kind],
            send.at[d, e, kind],
            recv.at[d, e, kind],
            d,
            ends[e],
        )

    def arrival(d, e, kind):
        return remote(
            partial.at[kind, ends[0], :, part(d)],
            out.at[sides[d], e, kind],
            send.at[d, e, kind],
            recv.at[d, e, kind],
            d,
            ends[e],
        )

    across = [
        remote(
            partial.at[kind, near_far], theirs.at[kind], p_send.at[kind], p_recv.at[kind], 0, near
        )
        for kind in range(kinds)
    ]
    bases = [
        remote(
            gathered.at[k, sides[1], :, g], base.at[k], base_send.at[k], base_recv.at[k], 1, g
        )
        for k in range(groups)
    ]
    sent = [final(1, 0, kind) for kind in range(kinds)]
    for copy in across + sent + bases:
        copy.start()
    mine = [
        pltpu.make_async_copy(
            partial.at[kind, g, :, part(0)], out.at[x, 0, kind], own_sem.at[kind]
        )
        for kind in range(kinds)
    ]
    for copy in mine:
        copy.start()
    for kind in range(kinds):
        across[kind].wait_recv()
        joined[kind] = (
            partial[kind, far].astype(jnp.float32) + theirs[kind].astype(jnp.float32)
        ).astype(jnp.bfloat16)
        for e in (2, 1):
            for d in range(2):
                copy = final(d, e, kind)
                copy.start()
                sent.append(copy)
    for copy in mine:
        copy.wait()
    for copy in across + sent:
        copy.wait_send()
    for kind in range(kinds):
        for d, e in steps:
            arrival(d, e, kind).wait_recv()
    for copy in bases:
        copy.wait()


def send_back(partial, gathered):
    groups, dp = gathered.shape[:2]
    kinds, _, half, width = gathered.shape[2:]
    feats = partial.shape[3] // dp
    dma = pltpu.SemaphoreType.DMA
    return pl.pallas_call(
        return_kernel,
        in_specs=[pl.BlockSpec(memory_space=pltpu.VMEM), pl.BlockSpec(memory_space=pl.ANY)],
        out_specs=[pl.BlockSpec(memory_space=pl.ANY)] * 2,
        out_shape=[
            jax.ShapeDtypeStruct((dp, 3, kinds, half, feats), partial.dtype),
            jax.ShapeDtypeStruct((groups, kinds, half, width), partial.dtype),
        ],
        scratch_shapes=[pltpu.VMEM((kinds, half, dp * feats), jnp.bfloat16) for _ in range(2)]
        + [dma((kinds,)) for _ in range(3)]
        + [dma((2, 3, kinds)), dma((2, 3, kinds)), dma((groups,)), dma((groups,))],
        cost_estimate=COMM_COST,
        compiler_params=pltpu.CompilerParams(collective_id=2, has_side_effects=True),
        name="send_back",
    )(partial, gathered)


def hidden_kernel(a, w, out, total):
    step = pl.program_id(1)
    left = jnp.concatenate([a[j, 0] for j in range(a.shape[0])], axis=1)
    depth, hid = left.shape[1], w.shape[4]
    product = jnp.dot(left, w[...].reshape(depth, hid), preferred_element_type=jnp.float32)

    @pl.when(step == 0)
    def _():
        total[...] = product

    @pl.when(step > 0)
    def _():
        total[...] += product

    @pl.when(step == pl.num_programs(1) - 1)
    def _():
        rows = total.shape[0] // 2
        value, tangent = gelu_pair(total[:rows], total[rows:])
        out[:rows] = value.astype(jnp.bfloat16)
        out[rows:] = tangent.astype(jnp.bfloat16)


def hidden_layer(gathered, w, dp):
    groups, _, rows, width = gathered.shape
    deep, hid = w.shape[3:]
    per = groups // dp
    return pl.pallas_call(
        hidden_kernel,
        grid=(dp, groups),
        in_specs=[
            pl.BlockSpec((dp, 1, rows, width), lambda f, k: (lax.rem(k, per), lax.div(k, per), 0, 0)),
            pl.BlockSpec((1, INNER, 1, deep, hid), lambda f, k: (f, 0, k, 0, 0)),
        ],
        out_specs=pl.BlockSpec((rows, hid), lambda f, k: (0, f)),
        out_shape=jax.ShapeDtypeStruct((rows, dp * hid), jnp.bfloat16),
        scratch_shapes=[pltpu.VMEM((rows, hid), jnp.float32)],
        cost_estimate=pl.CostEstimate(
            flops=2 * rows * groups * dp * width * dp * hid,
            bytes_accessed=2 * dp * INNER * groups * deep * hid,
            transcendentals=0,
        ),
        name="hidden_layer",
    )(gathered, w)


def in_layer(block, dp, seq):
    layers = [
        [d * seq + layer * INNER + i for d in range(dp) for i in range(INNER)]
        for layer in range(seq // INNER)
    ]
    return lax.all_gather(block, ("dp", "seq"), axis_index_groups=layers, axis=0, tiled=False)


def by_layers(query, key, value, d_query, d_key, d_value, residual, d_residual, w_in, w_out, dp, seq):
    groups = seq // INNER
    rows, feats = query.shape
    half, width = rows // dp, feats // groups
    w_out_layer = in_layer(w_out, dp, seq).reshape(dp * INNER * w_out.shape[0], w_out.shape[1])
    own, kv, win = spread(
        (query, d_query, residual, d_residual, key, value, d_key, d_value), w_in, groups
    )
    win, w_out_layer = lax.optimization_barrier((win, w_out_layer))
    w_in_layer = in_layer(win, dp, seq).reshape((dp, INNER) + win.shape)
    gathered = along_line(attend_wide(own, kv, dp), groups)
    hidden = hidden_layer(gathered.reshape(groups, dp, 2 * groups * half, width), w_in_layer, dp)
    partial = jnp.dot(hidden, w_out_layer, preferred_element_type=jnp.float32).astype(jnp.bfloat16)
    parts, base_other = send_back(partial.reshape(2, groups, half, dp * feats), gathered)
    x, g, _ = place(groups)
    base_own = lax.dynamic_index_in_dim(gathered, g, axis=3, keepdims=False)
    base_own = lax.dynamic_index_in_dim(base_own, x, axis=1, keepdims=False)
    base = jnp.stack([jnp.where(x == 0, base_own, base_other), jnp.where(x == 0, base_other, base_own)])
    base = base.transpose(0, 2, 3, 1, 4).reshape(2, 2, half, feats)
    total = base.astype(jnp.float32) + jnp.sum(parts.astype(jnp.float32), axis=1)
    out = total.astype(jnp.bfloat16).transpose(1, 0, 2, 3).reshape(2, rows, feats)
    return (out[0], out[1])


def on_device(*args, dp, seq):
    query, w_in = args[0], args[8]
    groups = seq // INNER
    tile = groups * HEAD_DIM
    if dp != 2 or seq % INNER or groups != 4 or query.shape[1] % tile or w_in.shape[1] % tile:
        return by_rows(*args)
    return by_layers(*args, dp=dp, seq=seq)


def solution(mesh):
    in_specs = (P("seq", "dp"),) * 9 + (P(("dp", "seq"), None),)
    out_specs = (P("seq", "dp"), P("seq", "dp"))
    body = functools.partial(on_device, dp=mesh.shape["dp"], seq=mesh.shape["seq"])
    return jax.shard_map(
        body, mesh=mesh, in_specs=in_specs, out_specs=out_specs, check_vma=False
    )
```
